128 devices in a mesh: ia: 4 (over y), ja: 16 (over z, x), ha: 2 (over core).
Axes of the slice: x: 4, y: 4, z: 4, core: 2. Of those that a mesh axis runs over, the one named last changes fastest.
Arguments:
- phase_space: float32 [6, 65536], P(None, ('ja', 'ha')), may hold values from -5 to 5
- derivatives: float32 [6, 65536], P(None, ('ja', 'ha')), may hold values from -8 to 8
- body_mass: float32 [65536], P(('ja', 'ha')), may hold values from 4.577637e-06 to 0.018310547
- active_lists: int32 [4, 4, 32], replicated, may hold values from -1 to 511, as said below
Outputs:
- phase_out: float32 [6, 65536], P(None, ('ja', 'ha'))
- deriv_out: float32 [6, 65536], P(None, ('ja', 'ha'))
The draws below stay inside these ranges and needn't reach their ends.
Inputs may be any that keep to these rules, and one draw needn't show every extreme that they name: `active_lists`: each block has a rung of 0 to 4 and is active in step s (1 to 4) exactly when s is a multiple of 2 ** (4 - rung). In each step a block id stands in at most one slot of one group, the live slots of a group come first, a group has at most 32 live slots, and in the last step every group has exactly 32.
All inputs are finite; a program needn't handle non-finite values.
Results may differ from the reference program's by a relative error of at most 0.0003.
Values sent between devices are 32-bit elements; how exact they have to be, the bound alone decides.
A program may use at most 64 MiB of HBM per device.

```python
import math
import jax
import jax.numpy as jnp
from jax import lax

BLK = 128
STEPS = 4
NBLK = 512
BODIES = 65536
CAP = 32
N_IA = 4


def draw_phase_space(key, part):
    key_radius, key_angle, key_height, key_kick = jax.random.split(key, 4)
    uniform_draw = jax.random.uniform(key_radius, (BODIES,), jnp.float32)
    radius = 0.6 + uniform_draw
    spread = 0.8
    azimuth = jax.random.uniform(key_angle, (BODIES,), jnp.float32, -math.pi, math.pi)
    height = 0.03 * jax.random.normal(key_height, (BODIES,), jnp.float32)
    velocity_kick = spread * jax.random.normal(key_kick, (3, BODIES), jnp.float32)
    orbit_speed = lax.rsqrt(radius)
    position = jnp.stack([radius * jnp.cos(azimuth), radius * jnp.sin(azimuth), height], axis=0)
    velocity = jnp.stack([-orbit_speed * jnp.sin(azimuth) + velocity_kick[0], orbit_speed * jnp.cos(azimuth) + velocity_kick[1], velocity_kick[2]], axis=0)
    return jnp.clip(jnp.concatenate([position, velocity], axis=0), -5.0, 5.0).astype(jnp.float32)


def draw_body_mass(key, part):
    key_small, key_big, key_pick = jax.random.split(jax.random.fold_in(key, 7), 3)
    small_log = jax.random.uniform(key_small, (BODIES,), jnp.float32, math.log(0.3), math.log(3.0))
    big_log = jax.random.uniform(key_big, (BODIES,), jnp.float32, math.log(120.0), math.log(1200.0))
    pick = jax.random.uniform(key_pick, (BODIES,), jnp.float32) < 0.02
    mass = jnp.exp(jnp.where(pick, big_log, small_log)) / BODIES
    return jnp.clip(mass, 0.3 / BODIES, 1200.0 / BODIES).astype(jnp.float32)


def draw_active_lists(key, part):
    key_pick, key_fine, key_coarse, key_order, key_groups = jax.random.split(key, 5)
    fine_count = N_IA * CAP
    chosen_order = jax.random.permutation(key_pick, NBLK).astype(jnp.int32)
    fine_rung = jax.random.randint(key_fine, (NBLK,), 2, 5)
    coarse_rung = jax.random.randint(key_coarse, (NBLK,), 0, 2)
    is_fine = jnp.zeros((NBLK,), jnp.int32).at[chosen_order[:fine_count]].set(1)
    rung_level = jnp.where(is_fine > 0, fine_rung, coarse_rung)
    period = jnp.power(2, 4 - rung_level).astype(jnp.int32)
    others = N_IA - 1
    tables = []
    for step_index in range(STEPS):
        active = (step_index + 1) % period == 0
        block_order = jax.random.permutation(jax.random.fold_in(key_order, step_index), NBLK).astype(jnp.int32)
        in_order = active[block_order].astype(jnp.int32)
        rank_order = jnp.cumsum(in_order) - 1
        group_order = jax.random.permutation(jax.random.fold_in(key_groups, step_index), N_IA).astype(jnp.int32)
        in_first = rank_order < CAP
        later_rank = jnp.maximum(rank_order - CAP, 0)
        group_index = jnp.where(in_first, group_order[0], group_order[1 + later_rank % others])
        slot_index = jnp.where(in_first, jnp.maximum(rank_order, 0), later_rank // others)
        group_index = jnp.where(in_order > 0, group_index, N_IA)
        slot_index = jnp.where(in_order > 0, slot_index, CAP)
        slot_table = jnp.full((N_IA, CAP), -1, jnp.int32).at[group_index, slot_index].set(block_order, mode='drop')
        tables.append(slot_table)
    return jnp.stack(tables, axis=0)


def steps_of(stream_key, extent, cuts, least, high):
    level = 1.0
    for axis_at, shards_of in cuts:
        steps = jax.random.uniform(jax.random.fold_in(jax.random.fold_in(stream_key, 6), axis_at), (shards_of,), jnp.float32, least / len(cuts), high / len(cuts))
        level = level * jnp.repeat(jnp.exp(steps), extent[axis_at] // shards_of).reshape((-1,) + (1,) * (len(extent) - 1 - axis_at))
    return level


def bell_draw(rng, shape, deviation, limit, cuts=(), kind=jnp.bfloat16):
    result = jax.random.normal(rng, shape, jnp.float32) * deviation
    if len(cuts) > 0:
        result = steps_of(rng, shape, cuts, -0.22, 0.18) * result
    return jnp.clip(result, min=-limit, max=limit).astype(kind)


def setup_inputs(seed: int = 0) -> dict:
    keys = jax.random.split(jax.random.key(seed), 5)
    return {
        "phase_space": draw_phase_space(jax.random.fold_in(keys[4], 71), 0),
        "derivatives": bell_draw(keys[1], (6, BODIES), 2.0, 8.0, ((1, 32),), jnp.float32),
        "body_mass": draw_body_mass(jax.random.fold_in(keys[4], 71), 0),
        "active_lists": draw_active_lists(jax.random.fold_in(keys[4], 71), 0),
    }


time_step = 0.02
soften_sq = 0.0025

def predict(phase_space, derivatives, elapsed):
    position = phase_space[0:3]
    velocity = phase_space[3:6]
    acceleration = derivatives[0:3]
    jerk_old = derivatives[3:6]
    pos_next = position + elapsed * (velocity + elapsed * (acceleration * 0.5 + elapsed * jerk_old / 6.0))
    vel_next = velocity + elapsed * (acceleration + elapsed * jerk_old * 0.5)
    return jnp.concatenate([pos_next, vel_next], axis=0)

def pair_terms(targets, field_rows, body_mass):
    sep_x = field_rows[0][None, :] - targets[0][:, None]
    sep_y = field_rows[1][None, :] - targets[1][:, None]
    sep_z = field_rows[2][None, :] - targets[2][:, None]
    rel_x = field_rows[3][None, :] - targets[3][:, None]
    rel_y = field_rows[4][None, :] - targets[4][:, None]
    rel_z = field_rows[5][None, :] - targets[5][:, None]
    dist_sq = sep_x * sep_x + sep_y * sep_y + sep_z * sep_z + soften_sq
    inv_r = lax.rsqrt(dist_sq)
    inv_cube = body_mass[None, :] * inv_r * inv_r * inv_r
    radial = 3.0 * (sep_x * rel_x + sep_y * rel_y + sep_z * rel_z) * inv_r * inv_r
    return jnp.stack([lax.optimization_barrier(jnp.sum(inv_cube * sep_x, axis=1)), lax.optimization_barrier(jnp.sum(inv_cube * sep_y, axis=1)), lax.optimization_barrier(jnp.sum(inv_cube * sep_z, axis=1)), lax.optimization_barrier(jnp.sum(inv_cube * (rel_x - radial * sep_x), axis=1)), lax.optimization_barrier(jnp.sum(inv_cube * (rel_y - radial * sep_y), axis=1)), lax.optimization_barrier(jnp.sum(inv_cube * (rel_z - radial * sep_z), axis=1))], axis=0)

def star_terms(predicted):
    position = predicted[0:3]
    velocity = predicted[3:6]
    inv_r = lax.rsqrt(lax.optimization_barrier(jnp.sum(position * position, axis=0)))
    inv_cube = inv_r * inv_r * inv_r
    radial = 3.0 * lax.optimization_barrier(jnp.sum(position * velocity, axis=0)) * inv_r * inv_r
    accel = -inv_cube[None, :] * position
    jerk_star = -inv_cube[None, :] * (velocity - radial[None, :] * position)
    return jnp.concatenate([accel, jerk_star], axis=0)

def correct(phase_space, derivatives, fresh, elapsed):
    half_dt = 0.5 * elapsed
    twelfth = elapsed * elapsed / 12.0
    vel_new = phase_space[3:6] + half_dt * (derivatives[0:3] + fresh[0:3]) + twelfth * (derivatives[3:6] - fresh[3:6])
    pos_new = phase_space[0:3] + half_dt * (phase_space[3:6] + vel_new) + twelfth * (derivatives[0:3] - fresh[0:3])
    return jnp.concatenate([pos_new, vel_new], axis=0)

def reference(phase_space, derivatives, body_mass, active_lists):
    block_total = BODIES // BLK
    all_blocks = jnp.arange(block_total, dtype=jnp.int32)
    last_time = jnp.zeros((BODIES,), jnp.float32)
    for step_index in range(STEPS):
        now_time = (step_index + 1) * time_step
        elapsed = (now_time - last_time)[None, :]
        predicted = predict(phase_space, derivatives, elapsed)
        step_lists = active_lists[step_index].reshape(-1).astype(jnp.int32)
        active_flags = jnp.any(step_lists[:, None] == all_blocks[None, :], axis=0)
        is_live = step_lists >= 0
        safe_ids = jnp.clip(step_lists, 0, block_total - 1).astype(jnp.int32)
        tiles = predicted.reshape(6, block_total, BLK).transpose(1, 0, 2)
        slot_tiles = jnp.take(tiles, safe_ids, axis=0)
        slot_fresh = lax.map(lambda tile_rows: pair_terms(tile_rows, predicted, body_mass), slot_tiles)
        slot_fresh = jnp.where(is_live[:, None, None], slot_fresh, jnp.float32(0.0))
        fresh = jnp.zeros((block_total, 6, BLK), jnp.float32).at[safe_ids].add(slot_fresh)
        fresh = fresh.transpose(1, 0, 2).reshape(6, BODIES)
        fresh = fresh + star_terms(predicted)
        active = jnp.repeat(active_flags, BLK)[None, :]
        corrected = correct(phase_space, derivatives, fresh, elapsed)
        phase_space = jnp.where(active, corrected, phase_space)
        derivatives = jnp.where(active, fresh, derivatives)
        last_time = jnp.where(active[0], jnp.float32(now_time), last_time)
    return (phase_space, derivatives)
```

```python
import math

import jax
import jax.numpy as jnp
from jax import lax
from jax.sharding import PartitionSpec as P

BLK = 128
STEPS = 4


time_step = 0.02
soften_sq = 0.0025


def predict(phase_space, derivatives, elapsed):
    position = phase_space[0:3]
    velocity = phase_space[3:6]
    acceleration = derivatives[0:3]
    jerk_old = derivatives[3:6]
    pos_next = position + elapsed * (
        velocity + elapsed * (acceleration * 0.5 + elapsed * jerk_old / 6.0)
    )
    vel_next = velocity + elapsed * (acceleration + elapsed * jerk_old * 0.5)
    return jnp.concatenate([pos_next, vel_next], axis=0)


def pair_terms(targets, field_rows, body_mass):
    sep_x = field_rows[0][None, :] - targets[0][:, None]
    sep_y = field_rows[1][None, :] - targets[1][:, None]
    sep_z = field_rows[2][None, :] - targets[2][:, None]
    rel_x = field_rows[3][None, :] - targets[3][:, None]
    rel_y = field_rows[4][None, :] - targets[4][:, None]
    rel_z = field_rows[5][None, :] - targets[5][:, None]
    dist_sq = sep_x * sep_x + sep_y * sep_y + sep_z * sep_z + soften_sq
    inv_r = lax.rsqrt(dist_sq)
    inv_cube = body_mass[None, :] * inv_r * inv_r * inv_r
    radial = 3.0 * (sep_x * rel_x + sep_y * rel_y + sep_z * rel_z) * inv_r * inv_r
    return jnp.stack(
        [
            jnp.sum(inv_cube * sep_x, axis=1),
            jnp.sum(inv_cube * sep_y, axis=1),
            jnp.sum(inv_cube * sep_z, axis=1),
            jnp.sum(inv_cube * (rel_x - radial * sep_x), axis=1),
            jnp.sum(inv_cube * (rel_y - radial * sep_y), axis=1),
            jnp.sum(inv_cube * (rel_z - radial * sep_z), axis=1),
        ],
        axis=0,
    )


def star_terms(predicted):
    position = predicted[0:3]
    velocity = predicted[3:6]
    inv_r = lax.rsqrt(jnp.sum(position * position, axis=0))
    inv_cube = inv_r * inv_r * inv_r
    radial = 3.0 * jnp.sum(position * velocity, axis=0) * inv_r * inv_r
    accel = -inv_cube[None, :] * position
    jerk_star = -inv_cube[None, :] * (velocity - radial[None, :] * position)
    return jnp.concatenate([accel, jerk_star], axis=0)


def correct(phase_space, derivatives, fresh, elapsed):
    half_dt = 0.5 * elapsed
    twelfth = elapsed * elapsed / 12.0
    vel_new = (
        phase_space[3:6]
        + half_dt * (derivatives[0:3] + fresh[0:3])
        + twelfth * (derivatives[3:6] - fresh[3:6])
    )
    pos_new = (
        phase_space[0:3]
        + half_dt * (phase_space[3:6] + vel_new)
        + twelfth * (derivatives[0:3] - fresh[0:3])
    )
    return jnp.concatenate([pos_new, vel_new], axis=0)


def field_forces(targets, field_rows, body_mass, chunks=4):
    count = field_rows.shape[1]
    width = count // chunks
    rows = field_rows.reshape(6, chunks, width).transpose(1, 0, 2)
    masses = body_mass.reshape(chunks, width)
    parts = lax.map(lambda c: pair_terms(targets, c[0], c[1]), (rows, masses))
    return jnp.sum(parts, axis=0)


def shards(phase_space, derivatives, body_mass, active_lists):
    every = ("ia", "ja", "ha")
    plane = ("ja", "ha")
    local = jnp.concatenate([phase_space, derivatives, body_mass[None, :]], axis=0)
    full = lax.all_gather(local, plane, axis=1, tiled=True)
    phase = full[0:6]
    deriv = full[6:12]
    mass = full[12]
    total = phase.shape[1]
    block_total = total // BLK
    slots = active_lists.shape[1] * active_lists.shape[2]
    my_group = lax.axis_index("ia")
    my_slot = lax.axis_index("ja") * lax.axis_size("ha") + lax.axis_index("ha")
    all_blocks = jnp.arange(block_total, dtype=jnp.int32)
    last_blk = jnp.zeros((block_total,), jnp.float32)
    for step_index in range(STEPS):
        now_time = (step_index + 1) * time_step
        step_lists = active_lists[step_index]
        flat = step_lists.reshape(-1)
        elapsed_blk = now_time - last_blk
        elapsed = jnp.repeat(elapsed_blk, BLK)[None, :]
        predicted = predict(phase, deriv, elapsed)
        my_id = step_lists[my_group, my_slot]
        safe = jnp.clip(my_id, 0, block_total - 1)
        start = safe * BLK
        targets = lax.dynamic_slice_in_dim(predicted, start, BLK, axis=1)
        mutual = field_forces(targets, predicted, mass)
        fresh = mutual + star_terms(targets)
        own_phase = lax.dynamic_slice_in_dim(phase, start, BLK, axis=1)
        own_deriv = lax.dynamic_slice_in_dim(deriv, start, BLK, axis=1)
        own_elapsed = lax.dynamic_slice_in_dim(elapsed, start, BLK, axis=1)
        corrected = correct(own_phase, own_deriv, fresh, own_elapsed)
        packed = jnp.concatenate([corrected, fresh], axis=0)
        sent = jnp.broadcast_to(packed[None], (slots,) + packed.shape)
        got = lax.all_to_all(sent, every, 0, 0, tiled=True)
        ids = jnp.where(flat >= 0, flat, block_total)
        phase = (
            phase.reshape(6, block_total, BLK)
            .at[:, ids]
            .set(got[:, 0:6].transpose(1, 0, 2), mode="drop")
            .reshape(6, total)
        )
        deriv = (
            deriv.reshape(6, block_total, BLK)
            .at[:, ids]
            .set(got[:, 6:12].transpose(1, 0, 2), mode="drop")
            .reshape(6, total)
        )
        active_flags = jnp.any(flat[:, None] == all_blocks[None, :], axis=0)
        last_blk = jnp.where(active_flags, jnp.float32(now_time), last_blk)
    local_count = phase_space.shape[1]
    offset = my_slot * local_count
    phase_out = lax.dynamic_slice_in_dim(phase, offset, local_count, axis=1)
    deriv_out = lax.dynamic_slice_in_dim(deriv, offset, local_count, axis=1)
    return (phase_out, deriv_out)


def solution(mesh):
    return jax.shard_map(
        shards,
        mesh=mesh,
        in_specs=(P(None, ("ja", "ha")), P(None, ("ja", "ha")), P(("ja", "ha")), P()),
        out_specs=(P(None, ("ja", "ha")), P(None, ("ja", "ha"))),
        check_vma=False,
    )
```

```python
import math

import jax
import jax.numpy as jnp
from jax import lax
from jax.sharding import PartitionSpec as P
from jax.experimental import pallas as pl
from jax.experimental.pallas import tpu as pltpu

BLK = 128
STEPS = 4


time_step = 0.02
soften_sq = 0.0025


def predict(phase_space, derivatives, elapsed):
    position = phase_space[0:3]
    velocity = phase_space[3:6]
    acceleration = derivatives[0:3]
    jerk_old = derivatives[3:6]
    pos_next = position + elapsed * (
        velocity + elapsed * (acceleration * 0.5 + elapsed * jerk_old / 6.0)
    )
    vel_next = velocity + elapsed * (acceleration + elapsed * jerk_old * 0.5)
    return jnp.concatenate([pos_next, vel_next], axis=0)


def pair_terms(targets, field_rows, body_mass):
    sep_x = field_rows[0][:, None] - targets[0][None, :]
    sep_y = field_rows[1][:, None] - targets[1][None, :]
    sep_z = field_rows[2][:, None] - targets[2][None, :]
    rel_x = field_rows[3][:, None] - targets[3][None, :]
    rel_y = field_rows[4][:, None] - targets[4][None, :]
    rel_z = field_rows[5][:, None] - targets[5][None, :]
    dist_sq = sep_x * sep_x + sep_y * sep_y + sep_z * sep_z + soften_sq
    inv_r = lax.rsqrt(dist_sq)
    inv_cube = body_mass[:, None] * inv_r * inv_r * inv_r
    radial = 3.0 * (sep_x * rel_x + sep_y * rel_y + sep_z * rel_z) * inv_r * inv_r
    return jnp.stack(
        [
            jnp.sum(inv_cube * sep_x, axis=0),
            jnp.sum(inv_cube * sep_y, axis=0),
            jnp.sum(inv_cube * sep_z, axis=0),
            jnp.sum(inv_cube * (rel_x - radial * sep_x), axis=0),
            jnp.sum(inv_cube * (rel_y - radial * sep_y), axis=0),
            jnp.sum(inv_cube * (rel_z - radial * sep_z), axis=0),
        ],
        axis=0,
    )


def star_terms(predicted):
    position = predicted[0:3]
    velocity = predicted[3:6]
    inv_r = lax.rsqrt(jnp.sum(position * position, axis=0))
    inv_cube = inv_r * inv_r * inv_r
    radial = 3.0 * jnp.sum(position * velocity, axis=0) * inv_r * inv_r
    accel = -inv_cube[None, :] * position
    jerk_star = -inv_cube[None, :] * (velocity - radial[None, :] * position)
    return jnp.concatenate([accel, jerk_star], axis=0)


def correct(phase_space, derivatives, fresh, elapsed):
    half_dt = 0.5 * elapsed
    twelfth = elapsed * elapsed / 12.0
    vel_new = (
        phase_space[3:6]
        + half_dt * (derivatives[0:3] + fresh[0:3])
        + twelfth * (derivatives[3:6] - fresh[3:6])
    )
    pos_new = (
        phase_space[0:3]
        + half_dt * (phase_space[3:6] + vel_new)
        + twelfth * (derivatives[0:3] - fresh[0:3])
    )
    return jnp.concatenate([pos_new, vel_new], axis=0)


def field_forces(targets, field_rows, body_mass, first, count, chunks=4):
    width = field_rows.shape[1] // chunks

    def body(i, acc):
        at = (first + i) * width
        rows = lax.dynamic_slice_in_dim(field_rows, at, width, axis=1)
        masses = lax.dynamic_slice_in_dim(body_mass, at, width, axis=0)
        return acc + pair_terms(targets, rows, masses)

    return lax.fori_loop(0, count, body, jnp.zeros((6, targets.shape[1]), jnp.float32))


def shards(phase_space, derivatives, body_mass, active_lists):
    every = ("ia", "ja", "ha")
    plane = ("ja", "ha")
    chunks = 4
    local = jnp.concatenate([phase_space, derivatives, body_mass[None, :]], axis=0)
    full = lax.all_gather(local, plane, axis=1, tiled=True)
    total = full.shape[1]
    mass = full[12]
    phase = full[0:6]
    deriv = full[6:12]
    block_total = total // BLK
    slots = active_lists.shape[1] * active_lists.shape[2]
    my_unit = (
        lax.axis_index("ia") * lax.axis_size("ja") + lax.axis_index("ja")
    ) * lax.axis_size("ha") + lax.axis_index("ha")
    all_blocks = jnp.arange(block_total, dtype=jnp.int32)
    units = jnp.arange(slots, dtype=jnp.int32)
    last_blk = jnp.zeros((block_total,), jnp.float32)
    for step_index in range(STEPS):
        now_time = (step_index + 1) * time_step
        flat = active_lists[step_index].reshape(-1)
        live = flat >= 0
        live_count = jnp.sum(live.astype(jnp.int32))
        rank = jnp.cumsum(live.astype(jnp.int32)) - 1
        compact = (
            jnp.zeros((slots,), jnp.int32)
            .at[jnp.where(live, rank, slots)]
            .set(flat, mode="drop")
        )
        split = jnp.where(
            live_count * 4 <= slots, 4, jnp.where(live_count * 2 <= slots, 2, 1)
        ).astype(jnp.int32)
        elapsed_blk = now_time - last_blk
        elapsed = jnp.repeat(elapsed_blk, BLK)[None, :]
        predicted = predict(phase, deriv, elapsed)
        my_job = my_unit // split
        my_part = my_unit - my_job * split
        my_id = jnp.clip(compact[jnp.clip(my_job, 0, slots - 1)], 0, block_total - 1)
        span = chunks // split
        count = jnp.where(my_job < live_count, span, 0)
        targets = lax.dynamic_slice_in_dim(predicted, my_id * BLK, BLK, axis=1)
        partial = field_forces(targets, predicted, mass, my_part * span, count, chunks)
        sent = jnp.broadcast_to(partial[None], (slots,) + partial.shape)
        got = lax.all_to_all(sent, every, 0, 0, tiled=True)
        job_of = units // split
        owner = jnp.where(job_of < live_count, compact[jnp.clip(job_of, 0, slots - 1)], -1)
        onehot = (all_blocks[:, None] == owner[None, :]).astype(jnp.float32)
        mutual = jnp.einsum(
            "bu,ucl->cbl", onehot, got, precision=lax.Precision.HIGHEST,
            preferred_element_type=jnp.float32,
        ).reshape(6, total)
        fresh = mutual + star_terms(predicted)
        corrected = correct(phase, deriv, fresh, elapsed)
        active_flags = jnp.any(flat[:, None] == all_blocks[None, :], axis=0)
        active = jnp.repeat(active_flags, BLK)[None, :]
        phase = jnp.where(active, corrected, phase)
        deriv = jnp.where(active, fresh, deriv)
        last_blk = jnp.where(active_flags, jnp.float32(now_time), last_blk)
    local_count = phase_space.shape[1]
    offset = (lax.axis_index("ja") * lax.axis_size("ha") + lax.axis_index("ha")) * local_count
    phase_out = lax.dynamic_slice_in_dim(phase, offset, local_count, axis=1)
    deriv_out = lax.dynamic_slice_in_dim(deriv, offset, local_count, axis=1)
    return (phase_out, deriv_out)


def solution(mesh):
    return jax.shard_map(
        shards,
        mesh=mesh,
        in_specs=(P(None, ("ja", "ha")), P(None, ("ja", "ha")), P(("ja", "ha")), P()),
        out_specs=(P(None, ("ja", "ha")), P(None, ("ja", "ha"))),
        check_vma=False,
    )
```

```python
import math

import jax
import jax.numpy as jnp
from jax import lax
from jax.sharding import PartitionSpec as P
from jax.experimental import pallas as pl
from jax.experimental.pallas import tpu as pltpu

BLK = 128
STEPS = 4


time_step = 0.02
soften_sq = 0.0025


def predict(phase_space, derivatives, elapsed):
    position = phase_space[0:3]
    velocity = phase_space[3:6]
    acceleration = derivatives[0:3]
    jerk_old = derivatives[3:6]
    pos_next = position + elapsed * (
        velocity + elapsed * (acceleration * 0.5 + elapsed * jerk_old / 6.0)
    )
    vel_next = velocity + elapsed * (acceleration + elapsed * jerk_old * 0.5)
    return jnp.concatenate([pos_next, vel_next], axis=0)


def pair_terms(targets, field_rows, body_mass):
    sep_x = field_rows[0][:, None] - targets[0][None, :]
    sep_y = field_rows[1][:, None] - targets[1][None, :]
    sep_z = field_rows[2][:, None] - targets[2][None, :]
    rel_x = field_rows[3][:, None] - targets[3][None, :]
    rel_y = field_rows[4][:, None] - targets[4][None, :]
    rel_z = field_rows[5][:, None] - targets[5][None, :]
    dist_sq = sep_x * sep_x + sep_y * sep_y + sep_z * sep_z + soften_sq
    inv_r = lax.rsqrt(dist_sq)
    inv_cube = body_mass[:, None] * inv_r * inv_r * inv_r
    radial = 3.0 * (sep_x * rel_x + sep_y * rel_y + sep_z * rel_z) * inv_r * inv_r
    return jnp.stack(
        [
            jnp.sum(inv_cube * sep_x, axis=0),
            jnp.sum(inv_cube * sep_y, axis=0),
            jnp.sum(inv_cube * sep_z, axis=0),
            jnp.sum(inv_cube * (rel_x - radial * sep_x), axis=0),
            jnp.sum(inv_cube * (rel_y - radial * sep_y), axis=0),
            jnp.sum(inv_cube * (rel_z - radial * sep_z), axis=0),
        ],
        axis=0,
    )


def star_terms(predicted):
    position = predicted[0:3]
    velocity = predicted[3:6]
    inv_r = lax.rsqrt(jnp.sum(position * position, axis=0))
    inv_cube = inv_r * inv_r * inv_r
    radial = 3.0 * jnp.sum(position * velocity, axis=0) * inv_r * inv_r
    accel = -inv_cube[None, :] * position
    jerk_star = -inv_cube[None, :] * (velocity - radial[None, :] * position)
    return jnp.concatenate([accel, jerk_star], axis=0)


def correct(phase_space, derivatives, fresh, elapsed):
    half_dt = 0.5 * elapsed
    twelfth = elapsed * elapsed / 12.0
    vel_new = (
        phase_space[3:6]
        + half_dt * (derivatives[0:3] + fresh[0:3])
        + twelfth * (derivatives[3:6] - fresh[3:6])
    )
    pos_new = (
        phase_space[0:3]
        + half_dt * (phase_space[3:6] + vel_new)
        + twelfth * (derivatives[0:3] - fresh[0:3])
    )
    return jnp.concatenate([pos_new, vel_new], axis=0)


def predict_chunked(phase, deriv, elapsed):
    position = phase[:, 0:3]
    velocity = phase[:, 3:6]
    acceleration = deriv[:, 0:3]
    jerk_old = deriv[:, 3:6]
    pos_next = position + elapsed * (
        velocity + elapsed * (acceleration * 0.5 + elapsed * jerk_old / 6.0)
    )
    vel_next = velocity + elapsed * (acceleration + elapsed * jerk_old * 0.5)
    return jnp.concatenate([pos_next, vel_next], axis=1)


def star_chunked(predicted):
    position = predicted[:, 0:3]
    velocity = predicted[:, 3:6]
    inv_r = lax.rsqrt(jnp.sum(position * position, axis=1))
    inv_cube = inv_r * inv_r * inv_r
    radial = 3.0 * jnp.sum(position * velocity, axis=1) * inv_r * inv_r
    accel = -inv_cube[:, None, :] * position
    jerk_star = -inv_cube[:, None, :] * (velocity - radial[:, None, :] * position)
    return jnp.concatenate([accel, jerk_star], axis=1)


def correct_chunked(phase, deriv, fresh, elapsed):
    half_dt = 0.5 * elapsed
    twelfth = elapsed * elapsed / 12.0
    vel_new = (
        phase[:, 3:6]
        + half_dt * (deriv[:, 0:3] + fresh[:, 0:3])
        + twelfth * (deriv[:, 3:6] - fresh[:, 3:6])
    )
    pos_new = (
        phase[:, 0:3]
        + half_dt * (phase[:, 3:6] + vel_new)
        + twelfth * (deriv[:, 0:3] - fresh[:, 0:3])
    )
    return jnp.concatenate([pos_new, vel_new], axis=1)


def field_forces(targets, field_rows, body_mass, first, count):
    def body(i, acc):
        rows = lax.dynamic_index_in_dim(field_rows, first + i, 0, keepdims=False)
        masses = lax.dynamic_index_in_dim(body_mass, first + i, 0, keepdims=False)
        return acc + pair_terms(targets, rows, masses)

    return lax.fori_loop(0, count, body, jnp.zeros((6, targets.shape[1]), jnp.float32))


def shards(phase_space, derivatives, body_mass, active_lists):
    every = ("ia", "ja", "ha")
    plane = ("ja", "ha")
    chunks = 4
    local = jnp.concatenate([phase_space, derivatives, body_mass[None, :]], axis=0)
    full = lax.all_gather(local, plane, axis=1, tiled=True)
    total = full.shape[1]
    width = total // chunks
    per_chunk = width // BLK
    full = full.reshape(13, chunks, width).transpose(1, 0, 2)
    mass = full[:, 12]
    phase = full[:, 0:6]
    deriv = full[:, 6:12]
    block_total = total // BLK
    slots = active_lists.shape[1] * active_lists.shape[2]
    my_unit = (
        lax.axis_index("ia") * lax.axis_size("ja") + lax.axis_index("ja")
    ) * lax.axis_size("ha") + lax.axis_index("ha")
    all_blocks = jnp.arange(block_total, dtype=jnp.int32)
    units = jnp.arange(slots, dtype=jnp.int32)
    last_blk = jnp.zeros((block_total,), jnp.float32)
    for step_index in range(STEPS):
        now_time = (step_index + 1) * time_step
        flat = active_lists[step_index].reshape(-1)
        live = flat >= 0
        live_count = jnp.sum(live.astype(jnp.int32))
        rank = jnp.cumsum(live.astype(jnp.int32)) - 1
        compact = (
            jnp.zeros((slots,), jnp.int32)
            .at[jnp.where(live, rank, slots)]
            .set(flat, mode="drop")
        )
        split = jnp.where(
            live_count * 4 <= slots, 4, jnp.where(live_count * 2 <= slots, 2, 1)
        ).astype(jnp.int32)
        elapsed_blk = now_time - last_blk
        elapsed = jnp.repeat(elapsed_blk, BLK).reshape(chunks, 1, width)
        predicted = predict_chunked(phase, deriv, elapsed)
        my_job = my_unit // split
        my_part = my_unit - my_job * split
        my_id = jnp.clip(compact[jnp.clip(my_job, 0, slots - 1)], 0, block_total - 1)
        span = chunks // split
        count = jnp.where(my_job < live_count, span, 0)
        targets = lax.dynamic_slice(
            predicted, (my_id // per_chunk, 0, (my_id % per_chunk) * BLK), (1, 6, BLK)
        )[0]
        partial = field_forces(targets, predicted, mass, my_part * span, count)
        sent = jnp.broadcast_to(partial[None], (slots,) + partial.shape)
        got = lax.all_to_all(sent, every, 0, 0, tiled=True)
        job_of = units // split
        owner = jnp.where(job_of < live_count, compact[jnp.clip(job_of, 0, slots - 1)], -1)
        onehot = (all_blocks[:, None] == owner[None, :]).astype(jnp.float32)
        mutual = jnp.einsum(
            "kbu,ucl->kcbl", onehot.reshape(chunks, per_chunk, slots), got,
            precision=lax.Precision.HIGHEST, preferred_element_type=jnp.float32,
        ).reshape(chunks, 6, width)
        fresh = mutual + star_chunked(predicted)
        corrected = correct_chunked(phase, deriv, fresh, elapsed)
        active_flags = jnp.any(flat[:, None] == all_blocks[None, :], axis=0)
        active = jnp.repeat(active_flags, BLK).reshape(chunks, 1, width)
        phase = jnp.where(active, corrected, phase)
        deriv = jnp.where(active, fresh, deriv)
        last_blk = jnp.where(active_flags, jnp.float32(now_time), last_blk)
    local_count = phase_space.shape[1]
    offset = (lax.axis_index("ja") * lax.axis_size("ha") + lax.axis_index("ha")) * local_count
    at = (offset // width, 0, offset % width)
    phase_out = lax.dynamic_slice(phase, at, (1, 6, local_count))[0]
    deriv_out = lax.dynamic_slice(deriv, at, (1, 6, local_count))[0]
    return (phase_out, deriv_out)


def solution(mesh):
    return jax.shard_map(
        shards,
        mesh=mesh,
        in_specs=(P(None, ("ja", "ha")), P(None, ("ja", "ha")), P(("ja", "ha")), P()),
        out_specs=(P(None, ("ja", "ha")), P(None, ("ja", "ha"))),
        check_vma=False,
    )
```

```python
import math

import jax
import jax.numpy as jnp
from jax import lax
from jax.sharding import PartitionSpec as P
from jax.experimental import pallas as pl
from jax.experimental.pallas import tpu as pltpu
from jax.experimental import pallas as pl
from jax.experimental.pallas import tpu as pltpu

BLK = 128
STEPS = 4


time_step = 0.02
soften_sq = 0.0025


def predict(phase_space, derivatives, elapsed):
    position = phase_space[0:3]
    velocity = phase_space[3:6]
    acceleration = derivatives[0:3]
    jerk_old = derivatives[3:6]
    pos_next = position + elapsed * (
        velocity + elapsed * (acceleration * 0.5 + elapsed * jerk_old / 6.0)
    )
    vel_next = velocity + elapsed * (acceleration + elapsed * jerk_old * 0.5)
    return jnp.concatenate([pos_next, vel_next], axis=0)


def pair_terms(targets, field_rows, body_mass):
    sep_x = field_rows[0][:, None] - targets[0][None, :]
    sep_y = field_rows[1][:, None] - targets[1][None, :]
    sep_z = field_rows[2][:, None] - targets[2][None, :]
    rel_x = field_rows[3][:, None] - targets[3][None, :]
    rel_y = field_rows[4][:, None] - targets[4][None, :]
    rel_z = field_rows[5][:, None] - targets[5][None, :]
    dist_sq = sep_x * sep_x + sep_y * sep_y + sep_z * sep_z + soften_sq
    inv_r = lax.rsqrt(dist_sq)
    inv_cube = body_mass[:, None] * inv_r * inv_r * inv_r
    radial = 3.0 * (sep_x * rel_x + sep_y * rel_y + sep_z * rel_z) * inv_r * inv_r
    return jnp.stack(
        [
            jnp.sum(inv_cube * sep_x, axis=0),
            jnp.sum(inv_cube * sep_y, axis=0),
            jnp.sum(inv_cube * sep_z, axis=0),
            jnp.sum(inv_cube * (rel_x - radial * sep_x), axis=0),
            jnp.sum(inv_cube * (rel_y - radial * sep_y), axis=0),
            jnp.sum(inv_cube * (rel_z - radial * sep_z), axis=0),
        ],
        axis=0,
    )


def star_terms(predicted):
    position = predicted[0:3]
    velocity = predicted[3:6]
    inv_r = lax.rsqrt(jnp.sum(position * position, axis=0))
    inv_cube = inv_r * inv_r * inv_r
    radial = 3.0 * jnp.sum(position * velocity, axis=0) * inv_r * inv_r
    accel = -inv_cube[None, :] * position
    jerk_star = -inv_cube[None, :] * (velocity - radial[None, :] * position)
    return jnp.concatenate([accel, jerk_star], axis=0)


def correct(phase_space, derivatives, fresh, elapsed):
    half_dt = 0.5 * elapsed
    twelfth = elapsed * elapsed / 12.0
    vel_new = (
        phase_space[3:6]
        + half_dt * (derivatives[0:3] + fresh[0:3])
        + twelfth * (derivatives[3:6] - fresh[3:6])
    )
    pos_new = (
        phase_space[0:3]
        + half_dt * (phase_space[3:6] + vel_new)
        + twelfth * (derivatives[0:3] - fresh[0:3])
    )
    return jnp.concatenate([pos_new, vel_new], axis=0)


def _force_kernel(ctl_ref, tgt_ref, src_ref, mass_ref, out_ref):
    targets = tgt_ref.shape[2]
    for part in range(2):
        lo = ctl_ref[2 * part]
        hi = ctl_ref[2 * part + 1]

        def per_target(t, carry, part=part, lo=lo, hi=hi):
            tx = tgt_ref[part, 0, t]
            ty = tgt_ref[part, 1, t]
            tz = tgt_ref[part, 2, t]
            tu = tgt_ref[part, 3, t]
            tv = tgt_ref[part, 4, t]
            tw = tgt_ref[part, 5, t]

            def per_tile(s, acc):
                rows = pl.ds(pl.multiple_of(s * 8, 8), 8)
                sep_x = src_ref[0, rows, :] - tx
                sep_y = src_ref[1, rows, :] - ty
                sep_z = src_ref[2, rows, :] - tz
                rel_x = src_ref[3, rows, :] - tu
                rel_y = src_ref[4, rows, :] - tv
                rel_z = src_ref[5, rows, :] - tw
                dist_sq = sep_x * sep_x + sep_y * sep_y + sep_z * sep_z + soften_sq
                inv_r = lax.rsqrt(dist_sq)
                inv_cube = mass_ref[rows, :] * inv_r * inv_r * inv_r
                radial = 3.0 * (sep_x * rel_x + sep_y * rel_y + sep_z * rel_z) * inv_r * inv_r
                return (
                    acc[0] + inv_cube * sep_x,
                    acc[1] + inv_cube * sep_y,
                    acc[2] + inv_cube * sep_z,
                    acc[3] + inv_cube * (rel_x - radial * sep_x),
                    acc[4] + inv_cube * (rel_y - radial * sep_y),
                    acc[5] + inv_cube * (rel_z - radial * sep_z),
                )

            zero = jnp.zeros((8, 128), jnp.float32)
            acc = lax.fori_loop(lo, hi, per_tile, (zero,) * 6)
            for k in range(6):
                out_ref[part, k, pl.ds(t, 1), :] = jnp.sum(acc[k], axis=0, keepdims=True)
            return carry

        lax.fori_loop(0, targets, per_target, 0)


def kernel_forces(ranges, targets, field, masses):
    out = pl.pallas_call(
        _force_kernel,
        out_shape=jax.ShapeDtypeStruct((2, 6, targets.shape[2], 128), jnp.float32),
        in_specs=[
            pl.BlockSpec(memory_space=pltpu.MemorySpace.SMEM),
            pl.BlockSpec(memory_space=pltpu.MemorySpace.SMEM),
            pl.BlockSpec(memory_space=pltpu.MemorySpace.VMEM),
            pl.BlockSpec(memory_space=pltpu.MemorySpace.VMEM),
        ],
        out_specs=pl.BlockSpec(memory_space=pltpu.MemorySpace.VMEM),
    )(ranges, targets, field, masses)
    return jnp.sum(out, axis=3)


def shards(phase_space, derivatives, body_mass, active_lists):
    every = ("ia", "ja", "ha")
    plane = ("ja", "ha")
    local = jnp.concatenate([phase_space, derivatives, body_mass[None, :]], axis=0)
    full = lax.all_gather(local, plane, axis=1, tiled=True)
    total = full.shape[1]
    block_total = total // BLK
    full = full.reshape(13, block_total, BLK)
    mass = full[12]
    phase = full[0:6]
    deriv = full[6:12]
    tiles = block_total // 8
    slots = active_lists.shape[1] * active_lists.shape[2]
    devices = lax.axis_size("ia") * lax.axis_size("ja") * lax.axis_size("ha")
    my_unit = (
        lax.axis_index("ia") * lax.axis_size("ja") + lax.axis_index("ja")
    ) * lax.axis_size("ha") + lax.axis_index("ha")
    all_blocks = jnp.arange(block_total, dtype=jnp.int32)
    units = jnp.arange(devices, dtype=jnp.int32)
    last_blk = jnp.zeros((block_total,), jnp.float32)
    for step_index in range(STEPS):
        now_time = (step_index + 1) * time_step
        flat = active_lists[step_index].reshape(-1)
        live = flat >= 0
        live_count = jnp.sum(live.astype(jnp.int32))
        rank = jnp.cumsum(live.astype(jnp.int32)) - 1
        compact = (
            jnp.zeros((slots,), jnp.int32)
            .at[jnp.where(live, rank, slots)]
            .set(flat, mode="drop")
        )
        work = live_count * tiles
        share = (work + devices - 1) // devices
        begin = jnp.minimum(units * share, work)
        finish = jnp.minimum(begin + share, work)
        job_a = jnp.minimum(begin // tiles, slots - 1)
        lo_a = begin - job_a * tiles
        hi_a = jnp.maximum(jnp.minimum(finish - job_a * tiles, tiles), lo_a)
        job_b = jnp.minimum(job_a + 1, slots - 1)
        hi_b = jnp.clip(finish - (job_a + 1) * tiles, 0, tiles)
        owner_a = jnp.where(hi_a > lo_a, compact[job_a], -1)
        owner_b = jnp.where(hi_b > 0, compact[job_b], -1)
        owner_all = jnp.stack([owner_a, owner_b], axis=1).reshape(-1)
        ranges = jnp.stack(
            [lo_a[my_unit], hi_a[my_unit], jnp.zeros_like(hi_b[my_unit]), hi_b[my_unit]]
        ).astype(jnp.int32)
        id_a = jnp.clip(compact[job_a[my_unit]], 0, block_total - 1)
        id_b = jnp.clip(compact[job_b[my_unit]], 0, block_total - 1)
        elapsed_blk = now_time - last_blk
        elapsed = elapsed_blk[None, :, None]
        predicted = predict(phase, deriv, elapsed)
        targets = jnp.stack(
            [
                lax.dynamic_index_in_dim(predicted, id_a, 1, keepdims=False),
                lax.dynamic_index_in_dim(predicted, id_b, 1, keepdims=False),
            ]
        )
        partial = kernel_forces(ranges, targets, predicted, mass)
        sent = jnp.broadcast_to(partial[None], (devices,) + partial.shape)
        got = lax.all_to_all(sent, every, 0, 0, tiled=True).reshape(2 * devices, 6, BLK)
        onehot = (all_blocks[:, None] == owner_all[None, :]).astype(jnp.float32)
        mutual = jnp.einsum(
            "bu,ucl->cbl", onehot, got,
            precision=lax.Precision.HIGHEST, preferred_element_type=jnp.float32,
        )
        fresh = mutual + star_terms(predicted)
        corrected = correct(phase, deriv, fresh, elapsed)
        active_flags = jnp.any(flat[:, None] == all_blocks[None, :], axis=0)
        active = active_flags[None, :, None]
        phase = jnp.where(active, corrected, phase)
        deriv = jnp.where(active, fresh, deriv)
        last_blk = jnp.where(active_flags, jnp.float32(now_time), last_blk)
    local_count = phase_space.shape[1]
    local_blocks = local_count // BLK
    offset = (lax.axis_index("ja") * lax.axis_size("ha") + lax.axis_index("ha")) * local_blocks
    phase_out = lax.dynamic_slice_in_dim(phase, offset, local_blocks, axis=1)
    deriv_out = lax.dynamic_slice_in_dim(deriv, offset, local_blocks, axis=1)
    return (phase_out.reshape(6, local_count), deriv_out.reshape(6, local_count))


def solution(mesh):
    return jax.shard_map(
        shards,
        mesh=mesh,
        in_specs=(P(None, ("ja", "ha")), P(None, ("ja", "ha")), P(("ja", "ha")), P()),
        out_specs=(P(None, ("ja", "ha")), P(None, ("ja", "ha"))),
        check_vma=False,
    )
```

```python
import math

import jax
import jax.numpy as jnp
from jax import lax
from jax.sharding import PartitionSpec as P
from jax.experimental import pallas as pl
from jax.experimental.pallas import tpu as pltpu
from jax.experimental import pallas as pl
from jax.experimental.pallas import tpu as pltpu

BLK = 128
GROUP = 8
STEPS = 4


time_step = 0.02
soften_sq = 0.0025


def predict(phase_space, derivatives, elapsed):
    position = phase_space[0:3]
    velocity = phase_space[3:6]
    acceleration = derivatives[0:3]
    jerk_old = derivatives[3:6]
    pos_next = position + elapsed * (
        velocity + elapsed * (acceleration * 0.5 + elapsed * jerk_old / 6.0)
    )
    vel_next = velocity + elapsed * (acceleration + elapsed * jerk_old * 0.5)
    return jnp.concatenate([pos_next, vel_next], axis=0)


def pair_terms(targets, field_rows, body_mass):
    sep_x = field_rows[0][:, None] - targets[0][None, :]
    sep_y = field_rows[1][:, None] - targets[1][None, :]
    sep_z = field_rows[2][:, None] - targets[2][None, :]
    rel_x = field_rows[3][:, None] - targets[3][None, :]
    rel_y = field_rows[4][:, None] - targets[4][None, :]
    rel_z = field_rows[5][:, None] - targets[5][None, :]
    dist_sq = sep_x * sep_x + sep_y * sep_y + sep_z * sep_z + soften_sq
    inv_r = lax.rsqrt(dist_sq)
    inv_cube = body_mass[:, None] * inv_r * inv_r * inv_r
    radial = 3.0 * (sep_x * rel_x + sep_y * rel_y + sep_z * rel_z) * inv_r * inv_r
    return jnp.stack(
        [
            jnp.sum(inv_cube * sep_x, axis=0),
            jnp.sum(inv_cube * sep_y, axis=0),
            jnp.sum(inv_cube * sep_z, axis=0),
            jnp.sum(inv_cube * (rel_x - radial * sep_x), axis=0),
            jnp.sum(inv_cube * (rel_y - radial * sep_y), axis=0),
            jnp.sum(inv_cube * (rel_z - radial * sep_z), axis=0),
        ],
        axis=0,
    )


def star_terms(predicted):
    position = predicted[0:3]
    velocity = predicted[3:6]
    inv_r = lax.rsqrt(jnp.sum(position * position, axis=0))
    inv_cube = inv_r * inv_r * inv_r
    radial = 3.0 * jnp.sum(position * velocity, axis=0) * inv_r * inv_r
    accel = -inv_cube[None, :] * position
    jerk_star = -inv_cube[None, :] * (velocity - radial[None, :] * position)
    return jnp.concatenate([accel, jerk_star], axis=0)


def correct(phase_space, derivatives, fresh, elapsed):
    half_dt = 0.5 * elapsed
    twelfth = elapsed * elapsed / 12.0
    vel_new = (
        phase_space[3:6]
        + half_dt * (derivatives[0:3] + fresh[0:3])
        + twelfth * (derivatives[3:6] - fresh[3:6])
    )
    pos_new = (
        phase_space[0:3]
        + half_dt * (phase_space[3:6] + vel_new)
        + twelfth * (derivatives[0:3] - fresh[0:3])
    )
    return jnp.concatenate([pos_new, vel_new], axis=0)


def _force_kernel(ctl_ref, tgt_ref, src_ref, mass_ref, out_ref):
    targets = tgt_ref.shape[2]
    for part in range(2):
        lo = ctl_ref[2 * part]
        hi = ctl_ref[2 * part + 1]

        def per_target(t, carry, part=part, lo=lo, hi=hi):
            tx = tgt_ref[part, 0, t]
            ty = tgt_ref[part, 1, t]
            tz = tgt_ref[part, 2, t]
            tu = tgt_ref[part, 3, t]
            tv = tgt_ref[part, 4, t]
            tw = tgt_ref[part, 5, t]

            def per_tile(s, acc):
                rows = pl.ds(pl.multiple_of(s * 8, 8), 8)
                sep_x = src_ref[0, rows, :] - tx
                sep_y = src_ref[1, rows, :] - ty
                sep_z = src_ref[2, rows, :] - tz
                rel_x = src_ref[3, rows, :] - tu
                rel_y = src_ref[4, rows, :] - tv
                rel_z = src_ref[5, rows, :] - tw
                dist_sq = sep_x * sep_x + sep_y * sep_y + sep_z * sep_z + soften_sq
                inv_r = lax.rsqrt(dist_sq)
                inv_cube = mass_ref[rows, :] * inv_r * inv_r * inv_r
                radial = 3.0 * (sep_x * rel_x + sep_y * rel_y + sep_z * rel_z) * inv_r * inv_r
                return (
                    acc[0] + inv_cube * sep_x,
                    acc[1] + inv_cube * sep_y,
                    acc[2] + inv_cube * sep_z,
                    acc[3] + inv_cube * (rel_x - radial * sep_x),
                    acc[4] + inv_cube * (rel_y - radial * sep_y),
                    acc[5] + inv_cube * (rel_z - radial * sep_z),
                )

            def per_group(g, acc):
                for k in range(GROUP):
                    acc = per_tile(g * GROUP + k, acc)
                return acc

            zero = jnp.zeros((8, 128), jnp.float32)
            acc = lax.fori_loop(lo, hi, per_group, (zero,) * 6)
            for k in range(6):
                out_ref[part, k, pl.ds(t, 1), :] = jnp.sum(acc[k], axis=0, keepdims=True)
            return carry

        lax.fori_loop(0, targets, per_target, 0)


def kernel_forces(ranges, targets, field, masses):
    out = pl.pallas_call(
        _force_kernel,
        out_shape=jax.ShapeDtypeStruct((2, 6, targets.shape[2], 128), jnp.float32),
        in_specs=[
            pl.BlockSpec(memory_space=pltpu.MemorySpace.SMEM),
            pl.BlockSpec(memory_space=pltpu.MemorySpace.SMEM),
            pl.BlockSpec(memory_space=pltpu.MemorySpace.VMEM),
            pl.BlockSpec(memory_space=pltpu.MemorySpace.VMEM),
        ],
        out_specs=pl.BlockSpec(memory_space=pltpu.MemorySpace.VMEM),
    )(ranges, targets, field, masses)
    return jnp.sum(out, axis=3)


def shards(phase_space, derivatives, body_mass, active_lists):
    every = ("ia", "ja", "ha")
    plane = ("ja", "ha")
    local = jnp.concatenate([phase_space, derivatives, body_mass[None, :]], axis=0)
    full = lax.all_gather(local, plane, axis=1, tiled=True)
    total = full.shape[1]
    block_total = total // BLK
    full = full.reshape(13, block_total, BLK)
    mass = full[12]
    phase = full[0:6]
    deriv = full[6:12]
    tiles = block_total // (8 * GROUP)
    slots = active_lists.shape[1] * active_lists.shape[2]
    devices = lax.axis_size("ia") * lax.axis_size("ja") * lax.axis_size("ha")
    my_unit = (
        lax.axis_index("ia") * lax.axis_size("ja") + lax.axis_index("ja")
    ) * lax.axis_size("ha") + lax.axis_index("ha")
    all_blocks = jnp.arange(block_total, dtype=jnp.int32)
    units = jnp.arange(devices, dtype=jnp.int32)
    last_blk = jnp.zeros((block_total,), jnp.float32)
    for step_index in range(STEPS):
        now_time = (step_index + 1) * time_step
        flat = active_lists[step_index].reshape(-1)
        live = flat >= 0
        live_count = jnp.sum(live.astype(jnp.int32))
        rank = jnp.cumsum(live.astype(jnp.int32)) - 1
        compact = (
            jnp.zeros((slots,), jnp.int32)
            .at[jnp.where(live, rank, slots)]
            .set(flat, mode="drop")
        )
        work = live_count * tiles
        share = (work + devices - 1) // devices
        begin = jnp.minimum(units * share, work)
        finish = jnp.minimum(begin + share, work)
        job_a = jnp.minimum(begin // tiles, slots - 1)
        lo_a = begin - job_a * tiles
        hi_a = jnp.maximum(jnp.minimum(finish - job_a * tiles, tiles), lo_a)
        job_b = jnp.minimum(job_a + 1, slots - 1)
        hi_b = jnp.clip(finish - (job_a + 1) * tiles, 0, tiles)
        owner_a = jnp.where(hi_a > lo_a, compact[job_a], -1)
        owner_b = jnp.where(hi_b > 0, compact[job_b], -1)
        owner_all = jnp.stack([owner_a, owner_b], axis=1).reshape(-1)
        ranges = jnp.stack(
            [lo_a[my_unit], hi_a[my_unit], jnp.zeros_like(hi_b[my_unit]), hi_b[my_unit]]
        ).astype(jnp.int32)
        id_a = jnp.clip(compact[job_a[my_unit]], 0, block_total - 1)
        id_b = jnp.clip(compact[job_b[my_unit]], 0, block_total - 1)
        elapsed_blk = now_time - last_blk
        elapsed = elapsed_blk[None, :, None]
        predicted = predict(phase, deriv, elapsed)
        targets = jnp.stack(
            [
                lax.dynamic_index_in_dim(predicted, id_a, 1, keepdims=False),
                lax.dynamic_index_in_dim(predicted, id_b, 1, keepdims=False),
            ]
        )
        partial = kernel_forces(ranges, targets, predicted, mass)
        sent = jnp.broadcast_to(partial[None], (devices,) + partial.shape)
        got = lax.all_to_all(sent, every, 0, 0, tiled=True).reshape(2 * devices, 6, BLK)
        onehot = (all_blocks[:, None] == owner_all[None, :]).astype(jnp.float32)
        mutual = jnp.einsum(
            "bu,ucl->cbl", onehot, got,
            precision=lax.Precision.HIGHEST, preferred_element_type=jnp.float32,
        )
        fresh = mutual + star_terms(predicted)
        corrected = correct(phase, deriv, fresh, elapsed)
        active_flags = jnp.any(flat[:, None] == all_blocks[None, :], axis=0)
        active = active_flags[None, :, None]
        phase = jnp.where(active, corrected, phase)
        deriv = jnp.where(active, fresh, deriv)
        last_blk = jnp.where(active_flags, jnp.float32(now_time), last_blk)
    local_count = phase_space.shape[1]
    local_blocks = local_count // BLK
    offset = (lax.axis_index("ja") * lax.axis_size("ha") + lax.axis_index("ha")) * local_blocks
    phase_out = lax.dynamic_slice_in_dim(phase, offset, local_blocks, axis=1)
    deriv_out = lax.dynamic_slice_in_dim(deriv, offset, local_blocks, axis=1)
    return (phase_out.reshape(6, local_count), deriv_out.reshape(6, local_count))


def solution(mesh):
    return jax.shard_map(
        shards,
        mesh=mesh,
        in_specs=(P(None, ("ja", "ha")), P(None, ("ja", "ha")), P(("ja", "ha")), P()),
        out_specs=(P(None, ("ja", "ha")), P(None, ("ja", "ha"))),
        check_vma=False,
    )
```

```python
import math

import jax
import jax.numpy as jnp
from jax import lax
from jax.sharding import PartitionSpec as P
from jax.experimental import pallas as pl
from jax.experimental.pallas import tpu as pltpu
from jax.experimental import pallas as pl
from jax.experimental.pallas import tpu as pltpu

BLK = 128
GROUP = 8
STEPS = 4


time_step = 0.02
soften_sq = 0.0025


def predict(phase_space, derivatives, elapsed):
    position = phase_space[0:3]
    velocity = phase_space[3:6]
    acceleration = derivatives[0:3]
    jerk_old = derivatives[3:6]
    pos_next = position + elapsed * (
        velocity + elapsed * (acceleration * 0.5 + elapsed * jerk_old / 6.0)
    )
    vel_next = velocity + elapsed * (acceleration + elapsed * jerk_old * 0.5)
    return jnp.concatenate([pos_next, vel_next], axis=0)


def pair_terms(targets, field_rows, body_mass):
    sep_x = field_rows[0][:, None] - targets[0][None, :]
    sep_y = field_rows[1][:, None] - targets[1][None, :]
    sep_z = field_rows[2][:, None] - targets[2][None, :]
    rel_x = field_rows[3][:, None] - targets[3][None, :]
    rel_y = field_rows[4][:, None] - targets[4][None, :]
    rel_z = field_rows[5][:, None] - targets[5][None, :]
    dist_sq = sep_x * sep_x + sep_y * sep_y + sep_z * sep_z + soften_sq
    inv_r = lax.rsqrt(dist_sq)
    inv_cube = body_mass[:, None] * inv_r * inv_r * inv_r
    radial = 3.0 * (sep_x * rel_x + sep_y * rel_y + sep_z * rel_z) * inv_r * inv_r
    return jnp.stack(
        [
            jnp.sum(inv_cube * sep_x, axis=0),
            jnp.sum(inv_cube * sep_y, axis=0),
            jnp.sum(inv_cube * sep_z, axis=0),
            jnp.sum(inv_cube * (rel_x - radial * sep_x), axis=0),
            jnp.sum(inv_cube * (rel_y - radial * sep_y), axis=0),
            jnp.sum(inv_cube * (rel_z - radial * sep_z), axis=0),
        ],
        axis=0,
    )


def star_terms(predicted):
    position = predicted[0:3]
    velocity = predicted[3:6]
    inv_r = lax.rsqrt(jnp.sum(position * position, axis=0))
    inv_cube = inv_r * inv_r * inv_r
    radial = 3.0 * jnp.sum(position * velocity, axis=0) * inv_r * inv_r
    accel = -inv_cube[None, :] * position
    jerk_star = -inv_cube[None, :] * (velocity - radial[None, :] * position)
    return jnp.concatenate([accel, jerk_star], axis=0)


def correct(phase_space, derivatives, fresh, elapsed):
    half_dt = 0.5 * elapsed
    twelfth = elapsed * elapsed / 12.0
    vel_new = (
        phase_space[3:6]
        + half_dt * (derivatives[0:3] + fresh[0:3])
        + twelfth * (derivatives[3:6] - fresh[3:6])
    )
    pos_new = (
        phase_space[0:3]
        + half_dt * (phase_space[3:6] + vel_new)
        + twelfth * (derivatives[0:3] - fresh[0:3])
    )
    return jnp.concatenate([pos_new, vel_new], axis=0)


def _force_kernel(ctl_ref, tgt_ref, src_ref, mass_ref, out_ref):
    targets = tgt_ref.shape[2]
    for part in range(2):
        lo = ctl_ref[2 * part]
        hi = ctl_ref[2 * part + 1]

        def per_target(t, carry, part=part, lo=lo, hi=hi):
            tx = tgt_ref[part, 0, t]
            ty = tgt_ref[part, 1, t]
            tz = tgt_ref[part, 2, t]
            tu = tgt_ref[part, 3, t]
            tv = tgt_ref[part, 4, t]
            tw = tgt_ref[part, 5, t]

            def per_tile(s, acc):
                rows = pl.ds(pl.multiple_of(s * 8, 8), 8)
                sep_x = src_ref[0, rows, :] - tx
                sep_y = src_ref[1, rows, :] - ty
                sep_z = src_ref[2, rows, :] - tz
                rel_x = src_ref[3, rows, :] - tu
                rel_y = src_ref[4, rows, :] - tv
                rel_z = src_ref[5, rows, :] - tw
                dist_sq = sep_x * sep_x + sep_y * sep_y + sep_z * sep_z + soften_sq
                inv_r = lax.rsqrt(dist_sq)
                inv_cube = mass_ref[rows, :] * inv_r * inv_r * inv_r
                radial = 3.0 * (sep_x * rel_x + sep_y * rel_y + sep_z * rel_z) * inv_r * inv_r
                return (
                    acc[0] + inv_cube * sep_x,
                    acc[1] + inv_cube * sep_y,
                    acc[2] + inv_cube * sep_z,
                    acc[3] + inv_cube * (rel_x - radial * sep_x),
                    acc[4] + inv_cube * (rel_y - radial * sep_y),
                    acc[5] + inv_cube * (rel_z - radial * sep_z),
                )

            def per_group(g, acc):
                for k in range(GROUP):
                    acc = per_tile(g * GROUP + k, acc)
                return acc

            zero = jnp.zeros((8, 128), jnp.float32)
            acc = lax.fori_loop(lo, hi, per_group, (zero,) * 6)
            for k in range(6):
                out_ref[part, k, pl.ds(t, 1), :] = jnp.sum(acc[k], axis=0, keepdims=True)
            return carry

        lax.fori_loop(0, targets, per_target, 0)


def kernel_forces(ranges, targets, field, masses):
    out = pl.pallas_call(
        _force_kernel,
        out_shape=jax.ShapeDtypeStruct((2, 6, targets.shape[2], 128), jnp.float32),
        in_specs=[
            pl.BlockSpec(memory_space=pltpu.MemorySpace.SMEM),
            pl.BlockSpec(memory_space=pltpu.MemorySpace.SMEM),
            pl.BlockSpec(memory_space=pltpu.MemorySpace.VMEM),
            pl.BlockSpec(memory_space=pltpu.MemorySpace.VMEM),
        ],
        out_specs=pl.BlockSpec(memory_space=pltpu.MemorySpace.VMEM),
    )(ranges, targets, field, masses)
    return jnp.sum(out, axis=3)


def shards(phase_space, derivatives, body_mass, active_lists):
    every = ("ia", "ja", "ha")
    plane = ("ja", "ha")
    local = jnp.concatenate([phase_space, derivatives, body_mass[None, :]], axis=0)
    full = lax.all_gather(local, plane, axis=1, tiled=True)
    total = full.shape[1]
    block_total = total // BLK
    full = full.reshape(13, block_total, BLK)
    tiles = block_total // (8 * GROUP)
    slots = active_lists.shape[1] * active_lists.shape[2]
    devices = lax.axis_size("ia") * lax.axis_size("ja") * lax.axis_size("ha")
    my_unit = (
        lax.axis_index("ia") * lax.axis_size("ja") + lax.axis_index("ja")
    ) * lax.axis_size("ha") + lax.axis_index("ha")
    all_blocks = jnp.arange(block_total, dtype=jnp.int32)
    units = jnp.arange(devices, dtype=jnp.int32)
    last_blk = jnp.zeros((block_total,), jnp.float32)
    plans = []
    for step_index in range(STEPS):
        flat = active_lists[step_index].reshape(-1)
        live = flat >= 0
        live_count = jnp.sum(live.astype(jnp.int32))
        rank = jnp.cumsum(live.astype(jnp.int32)) - 1
        compact = (
            jnp.zeros((slots,), jnp.int32)
            .at[jnp.where(live, rank, slots)]
            .set(flat, mode="drop")
        )
        work = live_count * tiles
        share = (work + devices - 1) // devices
        begin = jnp.minimum(units * share, work)
        finish = jnp.minimum(begin + share, work)
        job_a = jnp.minimum(begin // tiles, slots - 1)
        lo_a = begin - job_a * tiles
        hi_a = jnp.maximum(jnp.minimum(finish - job_a * tiles, tiles), lo_a)
        job_b = jnp.minimum(job_a + 1, slots - 1)
        hi_b = jnp.clip(finish - (job_a + 1) * tiles, 0, tiles)
        owner_a = jnp.where(hi_a > lo_a, compact[job_a], -1)
        owner_b = jnp.where(hi_b > 0, compact[job_b], -1)
        owner_all = jnp.stack([owner_a, owner_b], axis=1).reshape(-1)
        ranges = jnp.stack(
            [lo_a[my_unit], hi_a[my_unit], jnp.zeros_like(hi_b[my_unit]), hi_b[my_unit]]
        ).astype(jnp.int32)
        id_a = jnp.clip(compact[job_a[my_unit]], 0, block_total - 1)
        id_b = jnp.clip(compact[job_b[my_unit]], 0, block_total - 1)
        onehot = (all_blocks[:, None] == owner_all[None, :]).astype(jnp.float32)
        active_flags = jnp.any(flat[:, None] == all_blocks[None, :], axis=0)
        plans.append((ranges, id_a, id_b, onehot, active_flags))
    plans, full = lax.optimization_barrier((plans, full))
    mass = full[12]
    phase = full[0:6]
    deriv = full[6:12]
    for step_index in range(STEPS):
        now_time = (step_index + 1) * time_step
        ranges, id_a, id_b, onehot, active_flags = plans[step_index]
        elapsed_blk = now_time - last_blk
        elapsed = elapsed_blk[None, :, None]
        predicted = predict(phase, deriv, elapsed)
        targets = jnp.stack(
            [
                lax.dynamic_index_in_dim(predicted, id_a, 1, keepdims=False),
                lax.dynamic_index_in_dim(predicted, id_b, 1, keepdims=False),
            ]
        )
        partial = kernel_forces(ranges, targets, predicted, mass)
        sent = jnp.broadcast_to(partial[None], (devices,) + partial.shape)
        got = lax.all_to_all(sent, every, 0, 0, tiled=True).reshape(2 * devices, 6, BLK)
        mutual = jnp.einsum(
            "bu,ucl->cbl", onehot, got,
            precision=lax.Precision.HIGHEST, preferred_element_type=jnp.float32,
        )
        fresh = mutual + star_terms(predicted)
        corrected = correct(phase, deriv, fresh, elapsed)
        active = active_flags[None, :, None]
        phase = jnp.where(active, corrected, phase)
        deriv = jnp.where(active, fresh, deriv)
        last_blk = jnp.where(active_flags, jnp.float32(now_time), last_blk)
    local_count = phase_space.shape[1]
    local_blocks = local_count // BLK
    offset = (lax.axis_index("ja") * lax.axis_size("ha") + lax.axis_index("ha")) * local_blocks
    phase_out = lax.dynamic_slice_in_dim(phase, offset, local_blocks, axis=1)
    deriv_out = lax.dynamic_slice_in_dim(deriv, offset, local_blocks, axis=1)
    return (phase_out.reshape(6, local_count), deriv_out.reshape(6, local_count))


def solution(mesh):
    return jax.shard_map(
        shards,
        mesh=mesh,
        in_specs=(P(None, ("ja", "ha")), P(None, ("ja", "ha")), P(("ja", "ha")), P()),
        out_specs=(P(None, ("ja", "ha")), P(None, ("ja", "ha"))),
        check_vma=False,
    )
```

```python
import math

import jax
import jax.numpy as jnp
from jax import lax
from jax.sharding import PartitionSpec as P
from jax.experimental import pallas as pl
from jax.experimental.pallas import tpu as pltpu
from jax.experimental import pallas as pl
from jax.experimental.pallas import tpu as pltpu

BLK = 128
GROUP = 8
STEPS = 4


time_step = 0.02
soften_sq = 0.0025


def predict(phase_space, derivatives, elapsed):
    position = phase_space[0:3]
    velocity = phase_space[3:6]
    acceleration = derivatives[0:3]
    jerk_old = derivatives[3:6]
    pos_next = position + elapsed * (
        velocity + elapsed * (acceleration * 0.5 + elapsed * jerk_old / 6.0)
    )
    vel_next = velocity + elapsed * (acceleration + elapsed * jerk_old * 0.5)
    return jnp.concatenate([pos_next, vel_next], axis=0)


def pair_terms(targets, field_rows, body_mass):
    sep_x = field_rows[0][:, None] - targets[0][None, :]
    sep_y = field_rows[1][:, None] - targets[1][None, :]
    sep_z = field_rows[2][:, None] - targets[2][None, :]
    rel_x = field_rows[3][:, None] - targets[3][None, :]
    rel_y = field_rows[4][:, None] - targets[4][None, :]
    rel_z = field_rows[5][:, None] - targets[5][None, :]
    dist_sq = sep_x * sep_x + sep_y * sep_y + sep_z * sep_z + soften_sq
    inv_r = lax.rsqrt(dist_sq)
    inv_cube = body_mass[:, None] * inv_r * inv_r * inv_r
    radial = 3.0 * (sep_x * rel_x + sep_y * rel_y + sep_z * rel_z) * inv_r * inv_r
    return jnp.stack(
        [
            jnp.sum(inv_cube * sep_x, axis=0),
            jnp.sum(inv_cube * sep_y, axis=0),
            jnp.sum(inv_cube * sep_z, axis=0),
            jnp.sum(inv_cube * (rel_x - radial * sep_x), axis=0),
            jnp.sum(inv_cube * (rel_y - radial * sep_y), axis=0),
            jnp.sum(inv_cube * (rel_z - radial * sep_z), axis=0),
        ],
        axis=0,
    )


def star_terms(predicted):
    position = predicted[0:3]
    velocity = predicted[3:6]
    inv_r = lax.rsqrt(jnp.sum(position * position, axis=0))
    inv_cube = inv_r * inv_r * inv_r
    radial = 3.0 * jnp.sum(position * velocity, axis=0) * inv_r * inv_r
    accel = -inv_cube[None, :] * position
    jerk_star = -inv_cube[None, :] * (velocity - radial[None, :] * position)
    return jnp.concatenate([accel, jerk_star], axis=0)


def correct(phase_space, derivatives, fresh, elapsed):
    half_dt = 0.5 * elapsed
    twelfth = elapsed * elapsed / 12.0
    vel_new = (
        phase_space[3:6]
        + half_dt * (derivatives[0:3] + fresh[0:3])
        + twelfth * (derivatives[3:6] - fresh[3:6])
    )
    pos_new = (
        phase_space[0:3]
        + half_dt * (phase_space[3:6] + vel_new)
        + twelfth * (derivatives[0:3] - fresh[0:3])
    )
    return jnp.concatenate([pos_new, vel_new], axis=0)


def _force_kernel(ctl_ref, tgt_ref, src_ref, mass_ref, out_ref):
    targets = tgt_ref.shape[2]
    for part in range(2):
        lo = ctl_ref[2 * part]
        hi = ctl_ref[2 * part + 1]

        def per_target(t, carry, part=part, lo=lo, hi=hi):
            tx = tgt_ref[part, 0, t]
            ty = tgt_ref[part, 1, t]
            tz = tgt_ref[part, 2, t]
            tu = tgt_ref[part, 3, t]
            tv = tgt_ref[part, 4, t]
            tw = tgt_ref[part, 5, t]

            def per_tile(s, acc):
                rows = pl.ds(pl.multiple_of(s * 8, 8), 8)
                sep_x = src_ref[0, rows, :] - tx
                sep_y = src_ref[1, rows, :] - ty
                sep_z = src_ref[2, rows, :] - tz
                rel_x = src_ref[3, rows, :] - tu
                rel_y = src_ref[4, rows, :] - tv
                rel_z = src_ref[5, rows, :] - tw
                dist_sq = sep_x * sep_x + sep_y * sep_y + sep_z * sep_z + soften_sq
                inv_r = lax.rsqrt(dist_sq)
                inv_cube = mass_ref[rows, :] * inv_r * inv_r * inv_r
                radial = 3.0 * (sep_x * rel_x + sep_y * rel_y + sep_z * rel_z) * inv_r * inv_r
                return (
                    acc[0] + inv_cube * sep_x,
                    acc[1] + inv_cube * sep_y,
                    acc[2] + inv_cube * sep_z,
                    acc[3] + inv_cube * (rel_x - radial * sep_x),
                    acc[4] + inv_cube * (rel_y - radial * sep_y),
                    acc[5] + inv_cube * (rel_z - radial * sep_z),
                )

            def per_group(g, acc):
                for k in range(GROUP):
                    acc = per_tile(g * GROUP + k, acc)
                return acc

            zero = jnp.zeros((8, 128), jnp.float32)
            acc = lax.fori_loop(lo, hi, per_group, (zero,) * 6)
            for k in range(6):
                out_ref[part, k, pl.ds(t, 1), :] = jnp.sum(acc[k], axis=0, keepdims=True)
            return carry

        lax.fori_loop(0, targets, per_target, 0)


def kernel_forces(ranges, targets, field, masses):
    out = pl.pallas_call(
        _force_kernel,
        out_shape=jax.ShapeDtypeStruct((2, 6, targets.shape[2], 128), jnp.float32),
        in_specs=[
            pl.BlockSpec(memory_space=pltpu.MemorySpace.SMEM),
            pl.BlockSpec(memory_space=pltpu.MemorySpace.SMEM),
            pl.BlockSpec(memory_space=pltpu.MemorySpace.VMEM),
            pl.BlockSpec(memory_space=pltpu.MemorySpace.VMEM),
        ],
        out_specs=pl.BlockSpec(memory_space=pltpu.MemorySpace.VMEM),
    )(ranges, targets, field, masses)
    return jnp.sum(out, axis=3)


def shards(phase_space, derivatives, body_mass, active_lists):
    every = ("ia", "ja", "ha")
    plane = ("ja", "ha")
    local = jnp.concatenate([phase_space, derivatives, body_mass[None, :]], axis=0)
    full = lax.all_gather(local, plane, axis=1, tiled=True)
    total = full.shape[1]
    block_total = total // BLK
    full = full.reshape(13, block_total, BLK)
    mass = full[12]
    phase = full[0:6]
    deriv = full[6:12]
    tiles = block_total // (8 * GROUP)
    slots = active_lists.shape[1] * active_lists.shape[2]
    devices = lax.axis_size("ia") * lax.axis_size("ja") * lax.axis_size("ha")
    my_unit = (
        lax.axis_index("ia") * lax.axis_size("ja") + lax.axis_index("ja")
    ) * lax.axis_size("ha") + lax.axis_index("ha")
    all_blocks = jnp.arange(block_total, dtype=jnp.int32)
    units = jnp.arange(devices, dtype=jnp.int32)
    last_blk = jnp.zeros((block_total,), jnp.float32)
    times = jnp.array([(s + 1) * time_step for s in range(STEPS)], jnp.float32)

    def step(step_index, carry):
        phase, deriv, last_blk = carry
        now_time = times[step_index]
        flat = lax.dynamic_index_in_dim(active_lists, step_index, 0, keepdims=False).reshape(-1)
        live = flat >= 0
        live_count = jnp.sum(live.astype(jnp.int32))
        rank = jnp.cumsum(live.astype(jnp.int32)) - 1
        compact = (
            jnp.zeros((slots,), jnp.int32)
            .at[jnp.where(live, rank, slots)]
            .set(flat, mode="drop")
        )
        work = live_count * tiles
        share = (work + devices - 1) // devices
        begin = jnp.minimum(units * share, work)
        finish = jnp.minimum(begin + share, work)
        job_a = jnp.minimum(begin // tiles, slots - 1)
        lo_a = begin - job_a * tiles
        hi_a = jnp.maximum(jnp.minimum(finish - job_a * tiles, tiles), lo_a)
        job_b = jnp.minimum(job_a + 1, slots - 1)
        hi_b = jnp.clip(finish - (job_a + 1) * tiles, 0, tiles)
        owner_a = jnp.where(hi_a > lo_a, compact[job_a], -1)
        owner_b = jnp.where(hi_b > 0, compact[job_b], -1)
        owner_all = jnp.stack([owner_a, owner_b], axis=1).reshape(-1)
        ranges = jnp.stack(
            [lo_a[my_unit], hi_a[my_unit], jnp.zeros_like(hi_b[my_unit]), hi_b[my_unit]]
        ).astype(jnp.int32)
        id_a = jnp.clip(compact[job_a[my_unit]], 0, block_total - 1)
        id_b = jnp.clip(compact[job_b[my_unit]], 0, block_total - 1)
        elapsed_blk = now_time - last_blk
        elapsed = elapsed_blk[None, :, None]
        predicted = predict(phase, deriv, elapsed)
        targets = jnp.stack(
            [
                lax.dynamic_index_in_dim(predicted, id_a, 1, keepdims=False),
                lax.dynamic_index_in_dim(predicted, id_b, 1, keepdims=False),
            ]
        )
        partial = kernel_forces(ranges, targets, predicted, mass)
        sent = jnp.broadcast_to(partial[None], (devices,) + partial.shape)
        got = lax.all_to_all(sent, every, 0, 0, tiled=True).reshape(2 * devices, 6, BLK)
        onehot = (all_blocks[:, None] == owner_all[None, :]).astype(jnp.float32)
        mutual = jnp.einsum(
            "bu,ucl->cbl", onehot, got,
            precision=lax.Precision.HIGHEST, preferred_element_type=jnp.float32,
        )
        fresh = mutual + star_terms(predicted)
        corrected = correct(phase, deriv, fresh, elapsed)
        active_flags = jnp.any(flat[:, None] == all_blocks[None, :], axis=0)
        active = active_flags[None, :, None]
        phase = jnp.where(active, corrected, phase)
        deriv = jnp.where(active, fresh, deriv)
        last_blk = jnp.where(active_flags, now_time, last_blk)
        return phase, deriv, last_blk

    phase, deriv, last_blk = lax.fori_loop(0, STEPS, step, (phase, deriv, last_blk))
    local_count = phase_space.shape[1]
    local_blocks = local_count // BLK
    offset = (lax.axis_index("ja") * lax.axis_size("ha") + lax.axis_index("ha")) * local_blocks
    phase_out = lax.dynamic_slice_in_dim(phase, offset, local_blocks, axis=1)
    deriv_out = lax.dynamic_slice_in_dim(deriv, offset, local_blocks, axis=1)
    return (phase_out.reshape(6, local_count), deriv_out.reshape(6, local_count))


def solution(mesh):
    return jax.shard_map(
        shards,
        mesh=mesh,
        in_specs=(P(None, ("ja", "ha")), P(None, ("ja", "ha")), P(("ja", "ha")), P()),
        out_specs=(P(None, ("ja", "ha")), P(None, ("ja", "ha"))),
        check_vma=False,
    )
```

```python
import math

import jax
import jax.numpy as jnp
from jax import lax
from jax.sharding import PartitionSpec as P
from jax.experimental import pallas as pl
from jax.experimental.pallas import tpu as pltpu
from jax.experimental import pallas as pl
from jax.experimental.pallas import tpu as pltpu

BLK = 128
GROUP = 8
STEPS = 4


time_step = 0.02
soften_sq = 0.0025


def predict(phase_space, derivatives, elapsed):
    position = phase_space[0:3]
    velocity = phase_space[3:6]
    acceleration = derivatives[0:3]
    jerk_old = derivatives[3:6]
    pos_next = position + elapsed * (
        velocity + elapsed * (acceleration * 0.5 + elapsed * jerk_old / 6.0)
    )
    vel_next = velocity + elapsed * (acceleration + elapsed * jerk_old * 0.5)
    return jnp.concatenate([pos_next, vel_next], axis=0)


def pair_terms(targets, field_rows, body_mass):
    sep_x = field_rows[0][:, None] - targets[0][None, :]
    sep_y = field_rows[1][:, None] - targets[1][None, :]
    sep_z = field_rows[2][:, None] - targets[2][None, :]
    rel_x = field_rows[3][:, None] - targets[3][None, :]
    rel_y = field_rows[4][:, None] - targets[4][None, :]
    rel_z = field_rows[5][:, None] - targets[5][None, :]
    dist_sq = sep_x * sep_x + sep_y * sep_y + sep_z * sep_z + soften_sq
    inv_r = lax.rsqrt(dist_sq)
    inv_cube = body_mass[:, None] * inv_r * inv_r * inv_r
    radial = 3.0 * (sep_x * rel_x + sep_y * rel_y + sep_z * rel_z) * inv_r * inv_r
    return jnp.stack(
        [
            jnp.sum(inv_cube * sep_x, axis=0),
            jnp.sum(inv_cube * sep_y, axis=0),
            jnp.sum(inv_cube * sep_z, axis=0),
            jnp.sum(inv_cube * (rel_x - radial * sep_x), axis=0),
            jnp.sum(inv_cube * (rel_y - radial * sep_y), axis=0),
            jnp.sum(inv_cube * (rel_z - radial * sep_z), axis=0),
        ],
        axis=0,
    )


def star_terms(predicted):
    position = predicted[0:3]
    velocity = predicted[3:6]
    inv_r = lax.rsqrt(jnp.sum(position * position, axis=0))
    inv_cube = inv_r * inv_r * inv_r
    radial = 3.0 * jnp.sum(position * velocity, axis=0) * inv_r * inv_r
    accel = -inv_cube[None, :] * position
    jerk_star = -inv_cube[None, :] * (velocity - radial[None, :] * position)
    return jnp.concatenate([accel, jerk_star], axis=0)


def correct(phase_space, derivatives, fresh, elapsed):
    half_dt = 0.5 * elapsed
    twelfth = elapsed * elapsed / 12.0
    vel_new = (
        phase_space[3:6]
        + half_dt * (derivatives[0:3] + fresh[0:3])
        + twelfth * (derivatives[3:6] - fresh[3:6])
    )
    pos_new = (
        phase_space[0:3]
        + half_dt * (phase_space[3:6] + vel_new)
        + twelfth * (derivatives[0:3] - fresh[0:3])
    )
    return jnp.concatenate([pos_new, vel_new], axis=0)


def _force_kernel(ctl_ref, tgt_ref, src_ref, mass_ref, out_ref):
    targets = tgt_ref.shape[2]
    for part in range(2):
        lo = ctl_ref[2 * part]
        hi = ctl_ref[2 * part + 1]

        def per_target(t, carry, part=part, lo=lo, hi=hi):
            tx = tgt_ref[part, 0, t]
            ty = tgt_ref[part, 1, t]
            tz = tgt_ref[part, 2, t]
            tu = tgt_ref[part, 3, t]
            tv = tgt_ref[part, 4, t]
            tw = tgt_ref[part, 5, t]

            def per_tile(s, acc):
                rows = pl.ds(pl.multiple_of(s * 8, 8), 8)
                sep_x = src_ref[0, rows, :] - tx
                sep_y = src_ref[1, rows, :] - ty
                sep_z = src_ref[2, rows, :] - tz
                rel_x = src_ref[3, rows, :] - tu
                rel_y = src_ref[4, rows, :] - tv
                rel_z = src_ref[5, rows, :] - tw
                dist_sq = sep_x * sep_x + sep_y * sep_y + sep_z * sep_z + soften_sq
                inv_r = lax.rsqrt(dist_sq)
                inv_cube = mass_ref[rows, :] * inv_r * inv_r * inv_r
                radial = 3.0 * (sep_x * rel_x + sep_y * rel_y + sep_z * rel_z) * inv_r * inv_r
                return (
                    acc[0] + inv_cube * sep_x,
                    acc[1] + inv_cube * sep_y,
                    acc[2] + inv_cube * sep_z,
                    acc[3] + inv_cube * (rel_x - radial * sep_x),
                    acc[4] + inv_cube * (rel_y - radial * sep_y),
                    acc[5] + inv_cube * (rel_z - radial * sep_z),
                )

            def per_group(g, acc):
                for k in range(GROUP):
                    acc = per_tile(g * GROUP + k, acc)
                return acc

            zero = jnp.zeros((8, 128), jnp.float32)
            acc = lax.fori_loop(lo, hi, per_group, (zero,) * 6)
            for k in range(6):
                out_ref[part, k, pl.ds(t, 1), :] = jnp.sum(acc[k], axis=0, keepdims=True)
            return carry

        lax.fori_loop(0, targets, per_target, 0)


def kernel_forces(ranges, targets, field, masses):
    out = pl.pallas_call(
        _force_kernel,
        out_shape=jax.ShapeDtypeStruct((2, 6, targets.shape[2], 128), jnp.float32),
        in_specs=[
            pl.BlockSpec(memory_space=pltpu.MemorySpace.SMEM),
            pl.BlockSpec(memory_space=pltpu.MemorySpace.SMEM),
            pl.BlockSpec(memory_space=pltpu.MemorySpace.VMEM),
            pl.BlockSpec(memory_space=pltpu.MemorySpace.VMEM),
        ],
        out_specs=pl.BlockSpec(memory_space=pltpu.MemorySpace.VMEM),
    )(ranges, targets, field, masses)
    return jnp.sum(out, axis=3)


def shards(phase_space, derivatives, body_mass, active_lists):
    every = ("ia", "ja", "ha")
    plane = ("ja", "ha")
    local = jnp.concatenate([phase_space, derivatives, body_mass[None, :]], axis=0)
    full = lax.all_gather(local, plane, axis=1, tiled=True)
    total = full.shape[1]
    block_total = total // BLK
    full = full.reshape(13, block_total, BLK)
    tiles = block_total // (8 * GROUP)
    slots = active_lists.shape[1] * active_lists.shape[2]
    devices = lax.axis_size("ia") * lax.axis_size("ja") * lax.axis_size("ha")
    my_unit = (
        lax.axis_index("ia") * lax.axis_size("ja") + lax.axis_index("ja")
    ) * lax.axis_size("ha") + lax.axis_index("ha")
    all_blocks = jnp.arange(block_total, dtype=jnp.int32)
    units = jnp.arange(devices, dtype=jnp.int32)
    last_blk = jnp.zeros((block_total,), jnp.float32)
    flat = active_lists.reshape(active_lists.shape[0], -1)
    live = flat >= 0
    live_count = jnp.sum(live.astype(jnp.int32), axis=1, keepdims=True)
    rank = jnp.cumsum(live.astype(jnp.int32), axis=1) - 1
    picks = (rank[:, :, None] == units[None, None, :slots]) & live[:, :, None]
    compact = jnp.sum(jnp.where(picks, flat[:, :, None], 0), axis=1)
    work = live_count * tiles
    share = (work + devices - 1) // devices
    begin = jnp.minimum(units[None, :] * share, work)
    finish = jnp.minimum(begin + share, work)
    job_a = jnp.minimum(begin // tiles, slots - 1)
    lo_a = begin - job_a * tiles
    hi_a = jnp.maximum(jnp.minimum(finish - job_a * tiles, tiles), lo_a)
    job_b = jnp.minimum(job_a + 1, slots - 1)
    hi_b = jnp.clip(finish - (job_a + 1) * tiles, 0, tiles)
    owner_a = jnp.where(hi_a > lo_a, jnp.take_along_axis(compact, job_a, axis=1), -1)
    owner_b = jnp.where(hi_b > 0, jnp.take_along_axis(compact, job_b, axis=1), -1)
    owner_all = jnp.stack([owner_a, owner_b], axis=2).reshape(flat.shape[0], -1)
    onehots = (all_blocks[None, :, None] == owner_all[:, None, :]).astype(jnp.float32)
    active_all = jnp.any(flat[:, :, None] == all_blocks[None, None, :], axis=1)
    mine = lambda x: lax.dynamic_index_in_dim(x, my_unit, 1, keepdims=False)
    ranges_all = jnp.stack(
        [mine(lo_a), mine(hi_a), jnp.zeros_like(mine(hi_b)), mine(hi_b)], axis=1
    ).astype(jnp.int32)
    ids_all = jnp.clip(
        jnp.stack(
            [
                jnp.take_along_axis(compact, mine(job_a)[:, None], axis=1)[:, 0],
                jnp.take_along_axis(compact, mine(job_b)[:, None], axis=1)[:, 0],
            ],
            axis=1,
        ),
        0,
        block_total - 1,
    )
    plans = (ranges_all, ids_all, onehots, active_all)
    plans, full = lax.optimization_barrier((plans, full))
    ranges_all, ids_all, onehots, active_all = plans
    mass = full[12]
    phase = full[0:6]
    deriv = full[6:12]
    for step_index in range(STEPS):
        now_time = (step_index + 1) * time_step
        ranges = ranges_all[step_index]
        id_a = ids_all[step_index, 0]
        id_b = ids_all[step_index, 1]
        onehot = onehots[step_index]
        active_flags = active_all[step_index]
        elapsed_blk = now_time - last_blk
        elapsed = elapsed_blk[None, :, None]
        predicted = predict(phase, deriv, elapsed)
        targets = jnp.stack(
            [
                lax.dynamic_index_in_dim(predicted, id_a, 1, keepdims=False),
                lax.dynamic_index_in_dim(predicted, id_b, 1, keepdims=False),
            ]
        )
        partial = kernel_forces(ranges, targets, predicted, mass)
        sent = jnp.broadcast_to(partial[None], (devices,) + partial.shape)
        got = lax.all_to_all(sent, every, 0, 0, tiled=True).reshape(2 * devices, 6, BLK)
        mutual = jnp.einsum(
            "bu,ucl->cbl", onehot, got,
            precision=lax.Precision.HIGHEST, preferred_element_type=jnp.float32,
        )
        fresh = mutual + star_terms(predicted)
        corrected = correct(phase, deriv, fresh, elapsed)
        active = active_flags[None, :, None]
        phase = jnp.where(active, corrected, phase)
        deriv = jnp.where(active, fresh, deriv)
        last_blk = jnp.where(active_flags, jnp.float32(now_time), last_blk)
    local_count = phase_space.shape[1]
    local_blocks = local_count // BLK
    offset = (lax.axis_index("ja") * lax.axis_size("ha") + lax.axis_index("ha")) * local_blocks
    phase_out = lax.dynamic_slice_in_dim(phase, offset, local_blocks, axis=1)
    deriv_out = lax.dynamic_slice_in_dim(deriv, offset, local_blocks, axis=1)
    return (phase_out.reshape(6, local_count), deriv_out.reshape(6, local_count))


def solution(mesh):
    return jax.shard_map(
        shards,
        mesh=mesh,
        in_specs=(P(None, ("ja", "ha")), P(None, ("ja", "ha")), P(("ja", "ha")), P()),
        out_specs=(P(None, ("ja", "ha")), P(None, ("ja", "ha"))),
        check_vma=False,
    )
```

```python
import math

import jax
import jax.numpy as jnp
from jax import lax
from jax.sharding import PartitionSpec as P
from jax.experimental import pallas as pl
from jax.experimental.pallas import tpu as pltpu
from jax.experimental import pallas as pl
from jax.experimental.pallas import tpu as pltpu

BLK = 128
GROUP = 4
STEPS = 4


time_step = 0.02
soften_sq = 0.0025


def predict(phase_space, derivatives, elapsed):
    position = phase_space[0:3]
    velocity = phase_space[3:6]
    acceleration = derivatives[0:3]
    jerk_old = derivatives[3:6]
    pos_next = position + elapsed * (
        velocity + elapsed * (acceleration * 0.5 + elapsed * jerk_old / 6.0)
    )
    vel_next = velocity + elapsed * (acceleration + elapsed * jerk_old * 0.5)
    return jnp.concatenate([pos_next, vel_next], axis=0)


def pair_terms(targets, field_rows, body_mass):
    sep_x = field_rows[0][:, None] - targets[0][None, :]
    sep_y = field_rows[1][:, None] - targets[1][None, :]
    sep_z = field_rows[2][:, None] - targets[2][None, :]
    rel_x = field_rows[3][:, None] - targets[3][None, :]
    rel_y = field_rows[4][:, None] - targets[4][None, :]
    rel_z = field_rows[5][:, None] - targets[5][None, :]
    dist_sq = sep_x * sep_x + sep_y * sep_y + sep_z * sep_z + soften_sq
    inv_r = lax.rsqrt(dist_sq)
    inv_cube = body_mass[:, None] * inv_r * inv_r * inv_r
    radial = 3.0 * (sep_x * rel_x + sep_y * rel_y + sep_z * rel_z) * inv_r * inv_r
    return jnp.stack(
        [
            jnp.sum(inv_cube * sep_x, axis=0),
            jnp.sum(inv_cube * sep_y, axis=0),
            jnp.sum(inv_cube * sep_z, axis=0),
            jnp.sum(inv_cube * (rel_x - radial * sep_x), axis=0),
            jnp.sum(inv_cube * (rel_y - radial * sep_y), axis=0),
            jnp.sum(inv_cube * (rel_z - radial * sep_z), axis=0),
        ],
        axis=0,
    )


def star_terms(predicted):
    position = predicted[0:3]
    velocity = predicted[3:6]
    inv_r = lax.rsqrt(jnp.sum(position * position, axis=0))
    inv_cube = inv_r * inv_r * inv_r
    radial = 3.0 * jnp.sum(position * velocity, axis=0) * inv_r * inv_r
    accel = -inv_cube[None, :] * position
    jerk_star = -inv_cube[None, :] * (velocity - radial[None, :] * position)
    return jnp.concatenate([accel, jerk_star], axis=0)


def correct(phase_space, derivatives, fresh, elapsed):
    half_dt = 0.5 * elapsed
    twelfth = elapsed * elapsed / 12.0
    vel_new = (
        phase_space[3:6]
        + half_dt * (derivatives[0:3] + fresh[0:3])
        + twelfth * (derivatives[3:6] - fresh[3:6])
    )
    pos_new = (
        phase_space[0:3]
        + half_dt * (phase_space[3:6] + vel_new)
        + twelfth * (derivatives[0:3] - fresh[0:3])
    )
    return jnp.concatenate([pos_new, vel_new], axis=0)


def _force_kernel(ctl_ref, tgt_ref, src_ref, mass_ref, out_ref):
    targets = tgt_ref.shape[2]
    for part in range(2):
        lo = ctl_ref[2 * part]
        hi = ctl_ref[2 * part + 1]

        def per_target(t, carry, part=part, lo=lo, hi=hi):
            tx = tgt_ref[part, 0, t]
            ty = tgt_ref[part, 1, t]
            tz = tgt_ref[part, 2, t]
            tu = tgt_ref[part, 3, t]
            tv = tgt_ref[part, 4, t]
            tw = tgt_ref[part, 5, t]

            def per_tile(s, acc):
                rows = pl.ds(pl.multiple_of(s * 8, 8), 8)
                sep_x = src_ref[0, rows, :] - tx
                sep_y = src_ref[1, rows, :] - ty
                sep_z = src_ref[2, rows, :] - tz
                rel_x = src_ref[3, rows, :] - tu
                rel_y = src_ref[4, rows, :] - tv
                rel_z = src_ref[5, rows, :] - tw
                dist_sq = sep_x * sep_x + sep_y * sep_y + sep_z * sep_z + soften_sq
                inv_r = lax.rsqrt(dist_sq)
                inv_cube = mass_ref[rows, :] * inv_r * inv_r * inv_r
                radial = 3.0 * (sep_x * rel_x + sep_y * rel_y + sep_z * rel_z) * inv_r * inv_r
                return (
                    acc[0] + inv_cube * sep_x,
                    acc[1] + inv_cube * sep_y,
                    acc[2] + inv_cube * sep_z,
                    acc[3] + inv_cube * (rel_x - radial * sep_x),
                    acc[4] + inv_cube * (rel_y - radial * sep_y),
                    acc[5] + inv_cube * (rel_z - radial * sep_z),
                )

            def per_group(g, acc):
                for k in range(GROUP):
                    acc = per_tile(g * GROUP + k, acc)
                return acc

            zero = jnp.zeros((8, 128), jnp.float32)
            acc = lax.fori_loop(lo, hi, per_group, (zero,) * 6)
            for k in range(6):
                out_ref[part, k, pl.ds(t, 1), :] = jnp.sum(acc[k], axis=0, keepdims=True)
            return carry

        lax.fori_loop(0, targets, per_target, 0)


def kernel_forces(ranges, targets, field, masses):
    out = pl.pallas_call(
        _force_kernel,
        out_shape=jax.ShapeDtypeStruct((2, 6, targets.shape[2], 128), jnp.float32),
        in_specs=[
            pl.BlockSpec(memory_space=pltpu.MemorySpace.SMEM),
            pl.BlockSpec(memory_space=pltpu.MemorySpace.SMEM),
            pl.BlockSpec(memory_space=pltpu.MemorySpace.VMEM),
            pl.BlockSpec(memory_space=pltpu.MemorySpace.VMEM),
        ],
        out_specs=pl.BlockSpec(memory_space=pltpu.MemorySpace.VMEM),
    )(ranges, targets, field, masses)
    return jnp.sum(out, axis=3)


def shards(phase_space, derivatives, body_mass, active_lists):
    every = ("ia", "ja", "ha")
    plane = ("ja", "ha")
    local = jnp.concatenate([phase_space, derivatives, body_mass[None, :]], axis=0)
    full = lax.all_gather(local, plane, axis=1, tiled=True)
    total = full.shape[1]
    block_total = total // BLK
    full = full.reshape(13, block_total, BLK)
    tiles = block_total // (8 * GROUP)
    slots = active_lists.shape[1] * active_lists.shape[2]
    devices = lax.axis_size("ia") * lax.axis_size("ja") * lax.axis_size("ha")
    my_unit = (
        lax.axis_index("ia") * lax.axis_size("ja") + lax.axis_index("ja")
    ) * lax.axis_size("ha") + lax.axis_index("ha")
    all_blocks = jnp.arange(block_total, dtype=jnp.int32)
    units = jnp.arange(devices, dtype=jnp.int32)
    last_blk = jnp.zeros((block_total,), jnp.float32)
    flat = active_lists.reshape(active_lists.shape[0], -1)
    live = flat >= 0
    live_count = jnp.sum(live.astype(jnp.int32), axis=1, keepdims=True)
    rank = jnp.cumsum(live.astype(jnp.int32), axis=1) - 1
    picks = (rank[:, :, None] == units[None, None, :slots]) & live[:, :, None]
    compact = jnp.sum(jnp.where(picks, flat[:, :, None], 0), axis=1)
    work = live_count * tiles
    share = (work + devices - 1) // devices
    begin = jnp.minimum(units[None, :] * share, work)
    finish = jnp.minimum(begin + share, work)
    job_a = jnp.minimum(begin // tiles, slots - 1)
    lo_a = begin - job_a * tiles
    hi_a = jnp.maximum(jnp.minimum(finish - job_a * tiles, tiles), lo_a)
    job_b = jnp.minimum(job_a + 1, slots - 1)
    hi_b = jnp.clip(finish - (job_a + 1) * tiles, 0, tiles)
    owner_a = jnp.where(hi_a > lo_a, jnp.take_along_axis(compact, job_a, axis=1), -1)
    owner_b = jnp.where(hi_b > 0, jnp.take_along_axis(compact, job_b, axis=1), -1)
    owner_all = jnp.stack([owner_a, owner_b], axis=2).reshape(flat.shape[0], -1)
    onehots = (all_blocks[None, :, None] == owner_all[:, None, :]).astype(jnp.float32)
    active_all = jnp.any(flat[:, :, None] == all_blocks[None, None, :], axis=1)
    mine = lambda x: lax.dynamic_index_in_dim(x, my_unit, 1, keepdims=False)
    ranges_all = jnp.stack(
        [mine(lo_a), mine(hi_a), jnp.zeros_like(mine(hi_b)), mine(hi_b)], axis=1
    ).astype(jnp.int32)
    ids_all = jnp.clip(
        jnp.stack(
            [
                jnp.take_along_axis(compact, mine(job_a)[:, None], axis=1)[:, 0],
                jnp.take_along_axis(compact, mine(job_b)[:, None], axis=1)[:, 0],
            ],
            axis=1,
        ),
        0,
        block_total - 1,
    )
    plans = (ranges_all, ids_all, onehots, active_all)
    plans, full = lax.optimization_barrier((plans, full))
    ranges_all, ids_all, onehots, active_all = plans
    mass = full[12]
    phase = full[0:6]
    deriv = full[6:12]
    for step_index in range(STEPS):
        now_time = (step_index + 1) * time_step
        ranges = ranges_all[step_index]
        id_a = ids_all[step_index, 0]
        id_b = ids_all[step_index, 1]
        onehot = onehots[step_index]
        active_flags = active_all[step_index]
        elapsed_blk = now_time - last_blk
        elapsed = elapsed_blk[None, :, None]
        predicted = predict(phase, deriv, elapsed)
        targets = jnp.stack(
            [
                lax.dynamic_index_in_dim(predicted, id_a, 1, keepdims=False),
                lax.dynamic_index_in_dim(predicted, id_b, 1, keepdims=False),
            ]
        )
        partial = kernel_forces(ranges, targets, predicted, mass)
        sent = jnp.broadcast_to(partial[None], (devices,) + partial.shape)
        got = lax.all_to_all(sent, every, 0, 0, tiled=True).reshape(2 * devices, 6, BLK)
        mutual = jnp.einsum(
            "bu,ucl->cbl", onehot, got,
            precision=lax.Precision.HIGHEST, preferred_element_type=jnp.float32,
        )
        fresh = mutual + star_terms(predicted)
        corrected = correct(phase, deriv, fresh, elapsed)
        active = active_flags[None, :, None]
        phase = jnp.where(active, corrected, phase)
        deriv = jnp.where(active, fresh, deriv)
        last_blk = jnp.where(active_flags, jnp.float32(now_time), last_blk)
    local_count = phase_space.shape[1]
    local_blocks = local_count // BLK
    offset = (lax.axis_index("ja") * lax.axis_size("ha") + lax.axis_index("ha")) * local_blocks
    phase_out = lax.dynamic_slice_in_dim(phase, offset, local_blocks, axis=1)
    deriv_out = lax.dynamic_slice_in_dim(deriv, offset, local_blocks, axis=1)
    return (phase_out.reshape(6, local_count), deriv_out.reshape(6, local_count))


def solution(mesh):
    return jax.shard_map(
        shards,
        mesh=mesh,
        in_specs=(P(None, ("ja", "ha")), P(None, ("ja", "ha")), P(("ja", "ha")), P()),
        out_specs=(P(None, ("ja", "ha")), P(None, ("ja", "ha"))),
        check_vma=False,
    )
```

```python
import math

import jax
import jax.numpy as jnp
from jax import lax
from jax.sharding import PartitionSpec as P
from jax.experimental import pallas as pl
from jax.experimental.pallas import tpu as pltpu
from jax.experimental import pallas as pl
from jax.experimental.pallas import tpu as pltpu

BLK = 128
GROUP = 8
STEPS = 4


time_step = 0.02
soften_sq = 0.0025


def predict(phase_space, derivatives, elapsed):
    position = phase_space[0:3]
    velocity = phase_space[3:6]
    acceleration = derivatives[0:3]
    jerk_old = derivatives[3:6]
    pos_next = position + elapsed * (
        velocity + elapsed * (acceleration * 0.5 + elapsed * jerk_old / 6.0)
    )
    vel_next = velocity + elapsed * (acceleration + elapsed * jerk_old * 0.5)
    return jnp.concatenate([pos_next, vel_next], axis=0)


def pair_terms(targets, field_rows, body_mass):
    sep_x = field_rows[0][:, None] - targets[0][None, :]
    sep_y = field_rows[1][:, None] - targets[1][None, :]
    sep_z = field_rows[2][:, None] - targets[2][None, :]
    rel_x = field_rows[3][:, None] - targets[3][None, :]
    rel_y = field_rows[4][:, None] - targets[4][None, :]
    rel_z = field_rows[5][:, None] - targets[5][None, :]
    dist_sq = sep_x * sep_x + sep_y * sep_y + sep_z * sep_z + soften_sq
    inv_r = lax.rsqrt(dist_sq)
    inv_cube = body_mass[:, None] * inv_r * inv_r * inv_r
    radial = 3.0 * (sep_x * rel_x + sep_y * rel_y + sep_z * rel_z) * inv_r * inv_r
    return jnp.stack(
        [
            jnp.sum(inv_cube * sep_x, axis=0),
            jnp.sum(inv_cube * sep_y, axis=0),
            jnp.sum(inv_cube * sep_z, axis=0),
            jnp.sum(inv_cube * (rel_x - radial * sep_x), axis=0),
            jnp.sum(inv_cube * (rel_y - radial * sep_y), axis=0),
            jnp.sum(inv_cube * (rel_z - radial * sep_z), axis=0),
        ],
        axis=0,
    )


def star_terms(predicted):
    position = predicted[0:3]
    velocity = predicted[3:6]
    inv_r = lax.rsqrt(jnp.sum(position * position, axis=0))
    inv_cube = inv_r * inv_r * inv_r
    radial = 3.0 * jnp.sum(position * velocity, axis=0) * inv_r * inv_r
    accel = -inv_cube[None, :] * position
    jerk_star = -inv_cube[None, :] * (velocity - radial[None, :] * position)
    return jnp.concatenate([accel, jerk_star], axis=0)


def correct(phase_space, derivatives, fresh, elapsed):
    half_dt = 0.5 * elapsed
    twelfth = elapsed * elapsed / 12.0
    vel_new = (
        phase_space[3:6]
        + half_dt * (derivatives[0:3] + fresh[0:3])
        + twelfth * (derivatives[3:6] - fresh[3:6])
    )
    pos_new = (
        phase_space[0:3]
        + half_dt * (phase_space[3:6] + vel_new)
        + twelfth * (derivatives[0:3] - fresh[0:3])
    )
    return jnp.concatenate([pos_new, vel_new], axis=0)


def _force_kernel(ctl_ref, tgt_ref, src_ref, mass_ref, out_ref):
    targets = tgt_ref.shape[2]
    for part in range(2):
        lo = ctl_ref[2 * part]
        hi = ctl_ref[2 * part + 1]

        def per_target(t, carry, part=part, lo=lo, hi=hi):
            tx = tgt_ref[part, 0, t]
            ty = tgt_ref[part, 1, t]
            tz = tgt_ref[part, 2, t]
            tu = tgt_ref[part, 3, t]
            tv = tgt_ref[part, 4, t]
            tw = tgt_ref[part, 5, t]

            def per_tile(s, acc):
                rows = pl.ds(pl.multiple_of(s * 8, 8), 8)
                sep_x = src_ref[0, rows, :] - tx
                sep_y = src_ref[1, rows, :] - ty
                sep_z = src_ref[2, rows, :] - tz
                rel_x = src_ref[3, rows, :] - tu
                rel_y = src_ref[4, rows, :] - tv
                rel_z = src_ref[5, rows, :] - tw
                dist_sq = sep_x * sep_x + sep_y * sep_y + sep_z * sep_z + soften_sq
                inv_r = lax.rsqrt(dist_sq)
                inv_sq = inv_r * inv_r
                inv_cube = mass_ref[rows, :] * inv_sq * inv_r
                radial = (sep_x * rel_x + sep_y * rel_y + sep_z * rel_z) * inv_sq
                pull_x = inv_cube * sep_x
                pull_y = inv_cube * sep_y
                pull_z = inv_cube * sep_z
                return (
                    acc[0] + pull_x,
                    acc[1] + pull_y,
                    acc[2] + pull_z,
                    acc[3] + inv_cube * rel_x,
                    acc[4] + inv_cube * rel_y,
                    acc[5] + inv_cube * rel_z,
                    acc[6] + radial * pull_x,
                    acc[7] + radial * pull_y,
                    acc[8] + radial * pull_z,
                )

            def per_group(g, acc):
                for k in range(GROUP):
                    acc = per_tile(g * GROUP + k, acc)
                return acc

            zero = jnp.zeros((8, 128), jnp.float32)
            acc = lax.fori_loop(lo, hi, per_group, (zero,) * 9)
            for k in range(9):
                out_ref[part, k, pl.ds(t, 1), :] = jnp.sum(acc[k], axis=0, keepdims=True)
            return carry

        lax.fori_loop(0, targets, per_target, 0)


def kernel_forces(ranges, targets, field, masses):
    out = pl.pallas_call(
        _force_kernel,
        out_shape=jax.ShapeDtypeStruct((2, 9, targets.shape[2], 128), jnp.float32),
        in_specs=[
            pl.BlockSpec(memory_space=pltpu.MemorySpace.SMEM),
            pl.BlockSpec(memory_space=pltpu.MemorySpace.SMEM),
            pl.BlockSpec(memory_space=pltpu.MemorySpace.VMEM),
            pl.BlockSpec(memory_space=pltpu.MemorySpace.VMEM),
        ],
        out_specs=pl.BlockSpec(memory_space=pltpu.MemorySpace.VMEM),
    )(ranges, targets, field, masses)
    sums = jnp.sum(out, axis=3)
    return jnp.concatenate([sums[:, 0:3], sums[:, 3:6] - 3.0 * sums[:, 6:9]], axis=1)


def shards(phase_space, derivatives, body_mass, active_lists):
    every = ("ia", "ja", "ha")
    plane = ("ja", "ha")
    local = jnp.concatenate([phase_space, derivatives, body_mass[None, :]], axis=0)
    local = local.reshape(13, local.shape[1] // BLK, BLK)
    full = lax.all_gather(local, plane, axis=1, tiled=True)
    block_total = full.shape[1]
    tiles = block_total // (8 * GROUP)
    slots = active_lists.shape[1] * active_lists.shape[2]
    devices = lax.axis_size("ia") * lax.axis_size("ja") * lax.axis_size("ha")
    my_unit = (
        lax.axis_index("ia") * lax.axis_size("ja") + lax.axis_index("ja")
    ) * lax.axis_size("ha") + lax.axis_index("ha")
    all_blocks = jnp.arange(block_total, dtype=jnp.int32)
    units = jnp.arange(devices, dtype=jnp.int32)
    last_blk = jnp.zeros((block_total,), jnp.float32)
    flat = active_lists.reshape(active_lists.shape[0], -1)
    live = flat >= 0
    live_count = jnp.sum(live.astype(jnp.int32), axis=1, keepdims=True)
    rank = jnp.cumsum(live.astype(jnp.int32), axis=1) - 1
    picks = (rank[:, :, None] == units[None, None, :slots]) & live[:, :, None]
    compact = jnp.sum(jnp.where(picks, flat[:, :, None], 0), axis=1)
    work = live_count * tiles
    share = (work + devices - 1) // devices
    begin = jnp.minimum(units[None, :] * share, work)
    finish = jnp.minimum(begin + share, work)
    job_a = jnp.minimum(begin // tiles, slots - 1)
    lo_a = begin - job_a * tiles
    hi_a = jnp.maximum(jnp.minimum(finish - job_a * tiles, tiles), lo_a)
    job_b = jnp.minimum(job_a + 1, slots - 1)
    hi_b = jnp.clip(finish - (job_a + 1) * tiles, 0, tiles)
    owner_a = jnp.where(hi_a > lo_a, jnp.take_along_axis(compact, job_a, axis=1), -1)
    owner_b = jnp.where(hi_b > 0, jnp.take_along_axis(compact, job_b, axis=1), -1)
    owner_all = jnp.stack([owner_a, owner_b], axis=2).reshape(flat.shape[0], -1)
    onehots = (all_blocks[None, :, None] == owner_all[:, None, :]).astype(jnp.float32)
    active_all = jnp.any(flat[:, :, None] == all_blocks[None, None, :], axis=1)
    mine = lambda x: lax.dynamic_index_in_dim(x, my_unit, 1, keepdims=False)
    ranges_all = jnp.stack(
        [mine(lo_a), mine(hi_a), jnp.zeros_like(mine(hi_b)), mine(hi_b)], axis=1
    ).astype(jnp.int32)
    ids_all = jnp.clip(
        jnp.stack(
            [
                jnp.take_along_axis(compact, mine(job_a)[:, None], axis=1)[:, 0],
                jnp.take_along_axis(compact, mine(job_b)[:, None], axis=1)[:, 0],
            ],
            axis=1,
        ),
        0,
        block_total - 1,
    )
    plans = (ranges_all, ids_all, onehots, active_all)
    plans, full = lax.optimization_barrier((plans, full))
    ranges_all, ids_all, onehots, active_all = plans
    mass = full[12]
    phase = full[0:6]
    deriv = full[6:12]
    for step_index in range(STEPS):
        now_time = (step_index + 1) * time_step
        ranges = ranges_all[step_index]
        id_a = ids_all[step_index, 0]
        id_b = ids_all[step_index, 1]
        onehot = onehots[step_index]
        active_flags = active_all[step_index]
        elapsed_blk = now_time - last_blk
        elapsed = elapsed_blk[None, :, None]
        predicted = predict(phase, deriv, elapsed)
        targets = jnp.stack(
            [
                lax.dynamic_index_in_dim(predicted, id_a, 1, keepdims=False),
                lax.dynamic_index_in_dim(predicted, id_b, 1, keepdims=False),
            ]
        )
        partial = kernel_forces(ranges, targets, predicted, mass)
        sent = jnp.broadcast_to(partial[None], (devices,) + partial.shape)
        got = lax.all_to_all(sent, every, 0, 0, tiled=True).reshape(2 * devices, 6, BLK)
        mutual = jnp.einsum(
            "bu,ucl->cbl", onehot, got,
            precision=lax.Precision.HIGHEST, preferred_element_type=jnp.float32,
        )
        fresh = mutual + star_terms(predicted)
        corrected = correct(phase, deriv, fresh, elapsed)
        active = active_flags[None, :, None]
        phase = jnp.where(active, corrected, phase)
        deriv = jnp.where(active, fresh, deriv)
        last_blk = jnp.where(active_flags, jnp.float32(now_time), last_blk)
    local_count = phase_space.shape[1]
    local_blocks = local_count // BLK
    offset = (lax.axis_index("ja") * lax.axis_size("ha") + lax.axis_index("ha")) * local_blocks
    phase_out = lax.dynamic_slice_in_dim(phase, offset, local_blocks, axis=1)
    deriv_out = lax.dynamic_slice_in_dim(deriv, offset, local_blocks, axis=1)
    return (phase_out.reshape(6, local_count), deriv_out.reshape(6, local_count))


def solution(mesh):
    return jax.shard_map(
        shards,
        mesh=mesh,
        in_specs=(P(None, ("ja", "ha")), P(None, ("ja", "ha")), P(("ja", "ha")), P()),
        out_specs=(P(None, ("ja", "ha")), P(None, ("ja", "ha"))),
        check_vma=False,
    )
```

```python
import math

import jax
import jax.numpy as jnp
from jax import lax
from jax.sharding import PartitionSpec as P
from jax.experimental import pallas as pl
from jax.experimental.pallas import tpu as pltpu
from jax.experimental import pallas as pl
from jax.experimental.pallas import tpu as pltpu

BLK = 128
GROUP = 8
STEPS = 4


time_step = 0.02
soften_sq = 0.0025


def predict(phase_space, derivatives, elapsed):
    position = phase_space[0:3]
    velocity = phase_space[3:6]
    acceleration = derivatives[0:3]
    jerk_old = derivatives[3:6]
    pos_next = position + elapsed * (
        velocity + elapsed * (acceleration * 0.5 + elapsed * jerk_old / 6.0)
    )
    vel_next = velocity + elapsed * (acceleration + elapsed * jerk_old * 0.5)
    return jnp.concatenate([pos_next, vel_next], axis=0)


def pair_terms(targets, field_rows, body_mass):
    sep_x = field_rows[0][:, None] - targets[0][None, :]
    sep_y = field_rows[1][:, None] - targets[1][None, :]
    sep_z = field_rows[2][:, None] - targets[2][None, :]
    rel_x = field_rows[3][:, None] - targets[3][None, :]
    rel_y = field_rows[4][:, None] - targets[4][None, :]
    rel_z = field_rows[5][:, None] - targets[5][None, :]
    dist_sq = sep_x * sep_x + sep_y * sep_y + sep_z * sep_z + soften_sq
    inv_r = lax.rsqrt(dist_sq)
    inv_cube = body_mass[:, None] * inv_r * inv_r * inv_r
    radial = 3.0 * (sep_x * rel_x + sep_y * rel_y + sep_z * rel_z) * inv_r * inv_r
    return jnp.stack(
        [
            jnp.sum(inv_cube * sep_x, axis=0),
            jnp.sum(inv_cube * sep_y, axis=0),
            jnp.sum(inv_cube * sep_z, axis=0),
            jnp.sum(inv_cube * (rel_x - radial * sep_x), axis=0),
            jnp.sum(inv_cube * (rel_y - radial * sep_y), axis=0),
            jnp.sum(inv_cube * (rel_z - radial * sep_z), axis=0),
        ],
        axis=0,
    )


def star_terms(predicted):
    position = predicted[0:3]
    velocity = predicted[3:6]
    inv_r = lax.rsqrt(jnp.sum(position * position, axis=0))
    inv_cube = inv_r * inv_r * inv_r
    radial = 3.0 * jnp.sum(position * velocity, axis=0) * inv_r * inv_r
    accel = -inv_cube[None, :] * position
    jerk_star = -inv_cube[None, :] * (velocity - radial[None, :] * position)
    return jnp.concatenate([accel, jerk_star], axis=0)


def correct(phase_space, derivatives, fresh, elapsed):
    half_dt = 0.5 * elapsed
    twelfth = elapsed * elapsed / 12.0
    vel_new = (
        phase_space[3:6]
        + half_dt * (derivatives[0:3] + fresh[0:3])
        + twelfth * (derivatives[3:6] - fresh[3:6])
    )
    pos_new = (
        phase_space[0:3]
        + half_dt * (phase_space[3:6] + vel_new)
        + twelfth * (derivatives[0:3] - fresh[0:3])
    )
    return jnp.concatenate([pos_new, vel_new], axis=0)


def _force_kernel(ctl_ref, tgt_ref, src_ref, mass_ref, out_ref):
    targets = tgt_ref.shape[2]
    for part in range(2):
        lo = ctl_ref[2 * part]
        hi = ctl_ref[2 * part + 1]

        def per_target(t, carry, part=part, lo=lo, hi=hi):
            tx = tgt_ref[part, 0, t]
            ty = tgt_ref[part, 1, t]
            tz = tgt_ref[part, 2, t]
            tu = tgt_ref[part, 3, t]
            tv = tgt_ref[part, 4, t]
            tw = tgt_ref[part, 5, t]

            def per_tile(s, acc):
                rows = pl.ds(pl.multiple_of(s * 8, 8), 8)
                sep_x = src_ref[0, rows, :] - tx
                sep_y = src_ref[1, rows, :] - ty
                sep_z = src_ref[2, rows, :] - tz
                rel_x = src_ref[3, rows, :] - tu
                rel_y = src_ref[4, rows, :] - tv
                rel_z = src_ref[5, rows, :] - tw
                dist_sq = sep_x * sep_x + sep_y * sep_y + sep_z * sep_z + soften_sq
                inv_r = lax.rsqrt(dist_sq)
                inv_sq = inv_r * inv_r
                inv_cube = mass_ref[rows, :] * inv_sq * inv_r
                radial = (sep_x * rel_x + sep_y * rel_y + sep_z * rel_z) * inv_sq
                pull_x = inv_cube * sep_x
                pull_y = inv_cube * sep_y
                pull_z = inv_cube * sep_z
                return (
                    acc[0] + pull_x,
                    acc[1] + pull_y,
                    acc[2] + pull_z,
                    acc[3] + inv_cube * rel_x,
                    acc[4] + inv_cube * rel_y,
                    acc[5] + inv_cube * rel_z,
                    acc[6] + radial * pull_x,
                    acc[7] + radial * pull_y,
                    acc[8] + radial * pull_z,
                )

            def per_group(g, acc):
                for k in range(GROUP):
                    acc = per_tile(g * GROUP + k, acc)
                return acc

            zero = jnp.zeros((8, 128), jnp.float32)
            acc = lax.fori_loop(lo, hi, per_group, (zero,) * 9)
            for k in range(9):
                out_ref[part, k, pl.ds(t, 1), :] = jnp.sum(acc[k], axis=0, keepdims=True)
            return carry

        lax.fori_loop(0, targets, per_target, 0)


def kernel_forces(ranges, targets, field, masses):
    out = pl.pallas_call(
        _force_kernel,
        out_shape=jax.ShapeDtypeStruct((2, 9, targets.shape[2], 128), jnp.float32),
        in_specs=[
            pl.BlockSpec(memory_space=pltpu.MemorySpace.SMEM),
            pl.BlockSpec(memory_space=pltpu.MemorySpace.SMEM),
            pl.BlockSpec(memory_space=pltpu.MemorySpace.VMEM),
            pl.BlockSpec(memory_space=pltpu.MemorySpace.VMEM),
        ],
        out_specs=pl.BlockSpec(memory_space=pltpu.MemorySpace.VMEM),
    )(ranges, targets, field, masses)
    sums = jnp.sum(out, axis=3)
    return jnp.concatenate([sums[:, 0:3], sums[:, 3:6] - 3.0 * sums[:, 6:9]], axis=1)


def shards(phase_space, derivatives, body_mass, active_lists):
    every = ("ia", "ja", "ha")
    plane = ("ja", "ha")
    local = jnp.concatenate([phase_space, derivatives, body_mass[None, :]], axis=0)
    local = local.reshape(13, local.shape[1] // BLK, BLK)
    full = lax.all_gather(local, plane, axis=1, tiled=True)
    block_total = full.shape[1]
    tiles = block_total // (8 * GROUP)
    slots = active_lists.shape[1] * active_lists.shape[2]
    devices = lax.axis_size("ia") * lax.axis_size("ja") * lax.axis_size("ha")
    my_unit = (
        lax.axis_index("ia") * lax.axis_size("ja") + lax.axis_index("ja")
    ) * lax.axis_size("ha") + lax.axis_index("ha")
    all_blocks = jnp.arange(block_total, dtype=jnp.int32)
    units = jnp.arange(devices, dtype=jnp.int32)
    last_blk = jnp.zeros((block_total,), jnp.float32)
    flat = active_lists.reshape(active_lists.shape[0], -1)
    live = flat >= 0
    live_count = jnp.sum(live.astype(jnp.int32), axis=1, keepdims=True)
    rank = jnp.cumsum(live.astype(jnp.int32), axis=1) - 1
    picks = (rank[:, :, None] == units[None, None, :slots]) & live[:, :, None]
    compact = jnp.sum(jnp.where(picks, flat[:, :, None], 0), axis=1)
    work = live_count * tiles
    share = (work + devices - 1) // devices
    begin = jnp.minimum(units[None, :] * share, work)
    finish = jnp.minimum(begin + share, work)
    job_a = jnp.minimum(begin // tiles, slots - 1)
    lo_a = begin - job_a * tiles
    hi_a = jnp.maximum(jnp.minimum(finish - job_a * tiles, tiles), lo_a)
    job_b = jnp.minimum(job_a + 1, slots - 1)
    hi_b = jnp.clip(finish - (job_a + 1) * tiles, 0, tiles)
    owner_a = jnp.where(hi_a > lo_a, jnp.take_along_axis(compact, job_a, axis=1), -1)
    owner_b = jnp.where(hi_b > 0, jnp.take_along_axis(compact, job_b, axis=1), -1)
    owner_all = jnp.stack([owner_a, owner_b], axis=2).reshape(flat.shape[0], -1)
    onehots = (all_blocks[None, :, None] == owner_all[:, None, :]).astype(jnp.float32)
    active_all = jnp.any(flat[:, :, None] == all_blocks[None, None, :], axis=1)
    mine = lambda x: lax.dynamic_index_in_dim(x, my_unit, 1, keepdims=False)
    ranges_all = jnp.stack(
        [mine(lo_a), mine(hi_a), jnp.zeros_like(mine(hi_b)), mine(hi_b)], axis=1
    ).astype(jnp.int32)
    ids_all = jnp.clip(
        jnp.stack(
            [
                jnp.take_along_axis(compact, mine(job_a)[:, None], axis=1)[:, 0],
                jnp.take_along_axis(compact, mine(job_b)[:, None], axis=1)[:, 0],
            ],
            axis=1,
        ),
        0,
        block_total - 1,
    )
    plans = (ranges_all, ids_all, onehots, active_all)
    plans, full = lax.optimization_barrier((plans, full))
    ranges_all, ids_all, onehots, active_all = plans
    mass = full[12]
    phase = full[0:6]
    deriv = full[6:12]
    for step_index in range(STEPS):
        now_time = (step_index + 1) * time_step
        ranges = ranges_all[step_index]
        id_a = ids_all[step_index, 0]
        id_b = ids_all[step_index, 1]
        onehot = onehots[step_index]
        active_flags = active_all[step_index]
        elapsed_blk = now_time - last_blk
        elapsed = elapsed_blk[None, :, None]
        predicted = predict(phase, deriv, elapsed)
        targets = jnp.stack(
            [
                lax.dynamic_index_in_dim(predicted, id_a, 1, keepdims=False),
                lax.dynamic_index_in_dim(predicted, id_b, 1, keepdims=False),
            ]
        )
        partial = kernel_forces(ranges, targets, predicted, mass)
        sent = jnp.broadcast_to(partial[None], (devices,) + partial.shape)
        got = lax.all_to_all(sent, every, 0, 0, tiled=True).reshape(2 * devices, 6, BLK)
        if step_index == STEPS - 1:
            break
        mutual = jnp.einsum(
            "bu,ucl->cbl", onehot, got,
            precision=lax.Precision.HIGHEST, preferred_element_type=jnp.float32,
        )
        fresh = mutual + star_terms(predicted)
        corrected = correct(phase, deriv, fresh, elapsed)
        active = active_flags[None, :, None]
        phase = jnp.where(active, corrected, phase)
        deriv = jnp.where(active, fresh, deriv)
        last_blk = jnp.where(active_flags, jnp.float32(now_time), last_blk)
    local_count = phase_space.shape[1]
    local_blocks = local_count // BLK
    offset = (lax.axis_index("ja") * lax.axis_size("ha") + lax.axis_index("ha")) * local_blocks
    own = lambda x: lax.dynamic_slice_in_dim(x, offset, local_blocks, axis=1)
    mutual = jnp.einsum(
        "bu,ucl->cbl", lax.dynamic_slice_in_dim(onehot, offset, local_blocks, axis=0), got,
        precision=lax.Precision.HIGHEST, preferred_element_type=jnp.float32,
    )
    own_phase = own(phase)
    own_deriv = own(deriv)
    own_elapsed = own(elapsed)
    fresh = mutual + star_terms(own(predicted))
    corrected = correct(own_phase, own_deriv, fresh, own_elapsed)
    active = lax.dynamic_slice_in_dim(active_flags, offset, local_blocks)[None, :, None]
    phase_out = jnp.where(active, corrected, own_phase)
    deriv_out = jnp.where(active, fresh, own_deriv)
    return (phase_out.reshape(6, local_count), deriv_out.reshape(6, local_count))


def solution(mesh):
    return jax.shard_map(
        shards,
        mesh=mesh,
        in_specs=(P(None, ("ja", "ha")), P(None, ("ja", "ha")), P(("ja", "ha")), P()),
        out_specs=(P(None, ("ja", "ha")), P(None, ("ja", "ha"))),
        check_vma=False,
    )
```

```python
import math

import jax
import jax.numpy as jnp
from jax import lax
from jax.sharding import PartitionSpec as P
from jax.experimental import pallas as pl
from jax.experimental.pallas import tpu as pltpu
from jax.experimental import pallas as pl
from jax.experimental.pallas import tpu as pltpu

BLK = 128
GROUP = 8
STEPS = 4


time_step = 0.02
soften_sq = 0.0025


def predict(phase_space, derivatives, elapsed):
    position = phase_space[0:3]
    velocity = phase_space[3:6]
    acceleration = derivatives[0:3]
    jerk_old = derivatives[3:6]
    pos_next = position + elapsed * (
        velocity + elapsed * (acceleration * 0.5 + elapsed * jerk_old / 6.0)
    )
    vel_next = velocity + elapsed * (acceleration + elapsed * jerk_old * 0.5)
    return jnp.concatenate([pos_next, vel_next], axis=0)


def pair_terms(targets, field_rows, body_mass):
    sep_x = field_rows[0][:, None] - targets[0][None, :]
    sep_y = field_rows[1][:, None] - targets[1][None, :]
    sep_z = field_rows[2][:, None] - targets[2][None, :]
    rel_x = field_rows[3][:, None] - targets[3][None, :]
    rel_y = field_rows[4][:, None] - targets[4][None, :]
    rel_z = field_rows[5][:, None] - targets[5][None, :]
    dist_sq = sep_x * sep_x + sep_y * sep_y + sep_z * sep_z + soften_sq
    inv_r = lax.rsqrt(dist_sq)
    inv_cube = body_mass[:, None] * inv_r * inv_r * inv_r
    radial = 3.0 * (sep_x * rel_x + sep_y * rel_y + sep_z * rel_z) * inv_r * inv_r
    return jnp.stack(
        [
            jnp.sum(inv_cube * sep_x, axis=0),
            jnp.sum(inv_cube * sep_y, axis=0),
            jnp.sum(inv_cube * sep_z, axis=0),
            jnp.sum(inv_cube * (rel_x - radial * sep_x), axis=0),
            jnp.sum(inv_cube * (rel_y - radial * sep_y), axis=0),
            jnp.sum(inv_cube * (rel_z - radial * sep_z), axis=0),
        ],
        axis=0,
    )


def star_terms(predicted):
    position = predicted[0:3]
    velocity = predicted[3:6]
    inv_r = lax.rsqrt(jnp.sum(position * position, axis=0))
    inv_cube = inv_r * inv_r * inv_r
    radial = 3.0 * jnp.sum(position * velocity, axis=0) * inv_r * inv_r
    accel = -inv_cube[None, :] * position
    jerk_star = -inv_cube[None, :] * (velocity - radial[None, :] * position)
    return jnp.concatenate([accel, jerk_star], axis=0)


def correct(phase_space, derivatives, fresh, elapsed):
    half_dt = 0.5 * elapsed
    twelfth = elapsed * elapsed / 12.0
    vel_new = (
        phase_space[3:6]
        + half_dt * (derivatives[0:3] + fresh[0:3])
        + twelfth * (derivatives[3:6] - fresh[3:6])
    )
    pos_new = (
        phase_space[0:3]
        + half_dt * (phase_space[3:6] + vel_new)
        + twelfth * (derivatives[0:3] - fresh[0:3])
    )
    return jnp.concatenate([pos_new, vel_new], axis=0)


def _force_kernel(ctl_ref, tgt_ref, src_ref, mass_ref, out_ref):
    targets = tgt_ref.shape[2]
    for part in range(2):
        lo = ctl_ref[2 * part]
        hi = ctl_ref[2 * part + 1]

        def per_target(t, carry, part=part, lo=lo, hi=hi):
            tx = tgt_ref[part, 0, t]
            ty = tgt_ref[part, 1, t]
            tz = tgt_ref[part, 2, t]
            tu = tgt_ref[part, 3, t]
            tv = tgt_ref[part, 4, t]
            tw = tgt_ref[part, 5, t]

            def per_tile(s, acc):
                rows = pl.ds(pl.multiple_of(s * 8, 8), 8)
                sep_x = src_ref[0, rows, :] - tx
                sep_y = src_ref[1, rows, :] - ty
                sep_z = src_ref[2, rows, :] - tz
                rel_x = src_ref[3, rows, :] - tu
                rel_y = src_ref[4, rows, :] - tv
                rel_z = src_ref[5, rows, :] - tw
                dist_sq = sep_x * sep_x + sep_y * sep_y + sep_z * sep_z + soften_sq
                inv_r = lax.rsqrt(dist_sq)
                inv_sq = inv_r * inv_r
                inv_cube = mass_ref[rows, :] * inv_sq * inv_r
                radial = (sep_x * rel_x + sep_y * rel_y + sep_z * rel_z) * inv_sq
                pull_x = inv_cube * sep_x
                pull_y = inv_cube * sep_y
                pull_z = inv_cube * sep_z
                return (
                    acc[0] + pull_x,
                    acc[1] + pull_y,
                    acc[2] + pull_z,
                    acc[3] + inv_cube * rel_x,
                    acc[4] + inv_cube * rel_y,
                    acc[5] + inv_cube * rel_z,
                    acc[6] + radial * pull_x,
                    acc[7] + radial * pull_y,
                    acc[8] + radial * pull_z,
                )

            def per_group(g, acc):
                for k in range(GROUP):
                    acc = per_tile(g * GROUP + k, acc)
                return acc

            zero = jnp.zeros((8, 128), jnp.float32)
            acc = lax.fori_loop(lo, hi, per_group, (zero,) * 9)
            for k in range(9):
                out_ref[part, k, pl.ds(t, 1), :] = jnp.sum(acc[k], axis=0, keepdims=True)
            return carry

        lax.fori_loop(0, targets, per_target, 0)


def kernel_forces(ranges, targets, field, masses):
    out = pl.pallas_call(
        _force_kernel,
        out_shape=jax.ShapeDtypeStruct((2, 9, targets.shape[2], 128), jnp.float32),
        in_specs=[
            pl.BlockSpec(memory_space=pltpu.MemorySpace.SMEM),
            pl.BlockSpec(memory_space=pltpu.MemorySpace.SMEM),
            pl.BlockSpec(memory_space=pltpu.MemorySpace.VMEM),
            pl.BlockSpec(memory_space=pltpu.MemorySpace.VMEM),
        ],
        out_specs=pl.BlockSpec(memory_space=pltpu.MemorySpace.VMEM),
    )(ranges, targets, field, masses)
    sums = jnp.sum(out, axis=3)
    return jnp.concatenate([sums[:, 0:3], sums[:, 3:6] - 3.0 * sums[:, 6:9]], axis=1)


def shards(phase_space, derivatives, body_mass, active_lists):
    every = ("ia", "ja", "ha")
    plane = ("ja", "ha")
    local = jnp.concatenate([phase_space, derivatives, body_mass[None, :]], axis=0)
    local = local.reshape(13, local.shape[1] // BLK, BLK)
    full = lax.all_gather(local, plane, axis=1, tiled=True)
    block_total = full.shape[1]
    tiles = block_total // (8 * GROUP)
    slots = active_lists.shape[1] * active_lists.shape[2]
    devices = lax.axis_size("ia") * lax.axis_size("ja") * lax.axis_size("ha")
    my_unit = (
        lax.axis_index("ia") * lax.axis_size("ja") + lax.axis_index("ja")
    ) * lax.axis_size("ha") + lax.axis_index("ha")
    all_blocks = jnp.arange(block_total, dtype=jnp.int32)
    units = jnp.arange(devices, dtype=jnp.int32)
    last_blk = jnp.zeros((block_total,), jnp.float32)
    flat = active_lists.reshape(active_lists.shape[0], -1)
    live = flat >= 0
    live_count = jnp.sum(live.astype(jnp.int32), axis=1, keepdims=True)
    rank = jnp.cumsum(live.astype(jnp.int32), axis=1) - 1
    picks = (rank[:, :, None] == units[None, None, :slots]) & live[:, :, None]
    compact = jnp.sum(jnp.where(picks, flat[:, :, None], 0), axis=1)
    work = live_count * tiles
    share = (work + devices - 1) // devices
    begin = jnp.minimum(units[None, :] * share, work)
    finish = jnp.minimum(begin + share, work)
    job_a = jnp.minimum(begin // tiles, slots - 1)
    lo_a = begin - job_a * tiles
    hi_a = jnp.maximum(jnp.minimum(finish - job_a * tiles, tiles), lo_a)
    job_b = jnp.minimum(job_a + 1, slots - 1)
    hi_b = jnp.clip(finish - (job_a + 1) * tiles, 0, tiles)
    owner_a = jnp.where(hi_a > lo_a, jnp.take_along_axis(compact, job_a, axis=1), -1)
    owner_b = jnp.where(hi_b > 0, jnp.take_along_axis(compact, job_b, axis=1), -1)
    owner_all = jnp.stack([owner_a, owner_b], axis=2).reshape(flat.shape[0], -1)
    onehots = (all_blocks[None, :, None] == owner_all[:, None, :]).astype(jnp.float32)
    active_all = jnp.any(flat[:, :, None] == all_blocks[None, None, :], axis=1)
    mine = lambda x: lax.dynamic_index_in_dim(x, my_unit, 1, keepdims=False)
    ranges_all = jnp.stack(
        [mine(lo_a), mine(hi_a), jnp.zeros_like(mine(hi_b)), mine(hi_b)], axis=1
    ).astype(jnp.int32)
    ids_all = jnp.clip(
        jnp.stack(
            [
                jnp.take_along_axis(compact, mine(job_a)[:, None], axis=1)[:, 0],
                jnp.take_along_axis(compact, mine(job_b)[:, None], axis=1)[:, 0],
            ],
            axis=1,
        ),
        0,
        block_total - 1,
    )
    plans = (ranges_all, ids_all, onehots, active_all)
    plans, full = lax.optimization_barrier((plans, full))
    ranges_all, ids_all, onehots, active_all = plans
    mass = full[12]
    phase = full[0:6]
    deriv = full[6:12]
    for step_index in range(STEPS):
        now_time = (step_index + 1) * time_step
        ranges = ranges_all[step_index]
        id_a = ids_all[step_index, 0]
        id_b = ids_all[step_index, 1]
        onehot = onehots[step_index]
        active_flags = active_all[step_index]
        elapsed_blk = now_time - last_blk
        elapsed = elapsed_blk[None, :, None]
        predicted = predict(phase, deriv, elapsed)
        targets = jnp.stack(
            [
                lax.dynamic_index_in_dim(predicted, id_a, 1, keepdims=False),
                lax.dynamic_index_in_dim(predicted, id_b, 1, keepdims=False),
            ]
        )
        partial = kernel_forces(ranges, targets, predicted, mass)
        sent = jnp.broadcast_to(partial[None], (devices,) + partial.shape)
        got = lax.all_to_all(sent, every, 0, 0, tiled=True).reshape(2 * devices, 6, BLK)
        later, _ = lax.optimization_barrier((predicted, partial))
        if step_index == STEPS - 1:
            break
        mutual = jnp.einsum(
            "bu,ucl->cbl", onehot, got,
            precision=lax.Precision.HIGHEST, preferred_element_type=jnp.float32,
        )
        fresh = mutual + star_terms(later)
        corrected = correct(phase, deriv, fresh, elapsed)
        active = active_flags[None, :, None]
        phase = jnp.where(active, corrected, phase)
        deriv = jnp.where(active, fresh, deriv)
        last_blk = jnp.where(active_flags, jnp.float32(now_time), last_blk)
    local_count = phase_space.shape[1]
    local_blocks = local_count // BLK
    offset = (lax.axis_index("ja") * lax.axis_size("ha") + lax.axis_index("ha")) * local_blocks
    own = lambda x: lax.dynamic_slice_in_dim(x, offset, local_blocks, axis=1)
    mutual = jnp.einsum(
        "bu,ucl->cbl", lax.dynamic_slice_in_dim(onehot, offset, local_blocks, axis=0), got,
        precision=lax.Precision.HIGHEST, preferred_element_type=jnp.float32,
    )
    own_phase = own(phase)
    own_deriv = own(deriv)
    own_elapsed = own(elapsed)
    fresh = mutual + star_terms(own(later))
    corrected = correct(own_phase, own_deriv, fresh, own_elapsed)
    active = lax.dynamic_slice_in_dim(active_flags, offset, local_blocks)[None, :, None]
    phase_out = jnp.where(active, corrected, own_phase)
    deriv_out = jnp.where(active, fresh, own_deriv)
    return (phase_out.reshape(6, local_count), deriv_out.reshape(6, local_count))


def solution(mesh):
    return jax.shard_map(
        shards,
        mesh=mesh,
        in_specs=(P(None, ("ja", "ha")), P(None, ("ja", "ha")), P(("ja", "ha")), P()),
        out_specs=(P(None, ("ja", "ha")), P(None, ("ja", "ha"))),
        check_vma=False,
    )
```

```python
import math

import jax
import jax.numpy as jnp
from jax import lax
from jax.sharding import PartitionSpec as P
from jax.experimental import pallas as pl
from jax.experimental.pallas import tpu as pltpu
from jax.experimental import pallas as pl
from jax.experimental.pallas import tpu as pltpu

BLK = 128
GROUP = 8
STEPS = 4


time_step = 0.02
soften_sq = 0.0025


def predict(phase_space, derivatives, elapsed):
    position = phase_space[0:3]
    velocity = phase_space[3:6]
    acceleration = derivatives[0:3]
    jerk_old = derivatives[3:6]
    pos_next = position + elapsed * (
        velocity + elapsed * (acceleration * 0.5 + elapsed * jerk_old / 6.0)
    )
    vel_next = velocity + elapsed * (acceleration + elapsed * jerk_old * 0.5)
    return jnp.concatenate([pos_next, vel_next], axis=0)


def pair_terms(targets, field_rows, body_mass):
    sep_x = field_rows[0][:, None] - targets[0][None, :]
    sep_y = field_rows[1][:, None] - targets[1][None, :]
    sep_z = field_rows[2][:, None] - targets[2][None, :]
    rel_x = field_rows[3][:, None] - targets[3][None, :]
    rel_y = field_rows[4][:, None] - targets[4][None, :]
    rel_z = field_rows[5][:, None] - targets[5][None, :]
    dist_sq = sep_x * sep_x + sep_y * sep_y + sep_z * sep_z + soften_sq
    inv_r = lax.rsqrt(dist_sq)
    inv_cube = body_mass[:, None] * inv_r * inv_r * inv_r
    radial = 3.0 * (sep_x * rel_x + sep_y * rel_y + sep_z * rel_z) * inv_r * inv_r
    return jnp.stack(
        [
            jnp.sum(inv_cube * sep_x, axis=0),
            jnp.sum(inv_cube * sep_y, axis=0),
            jnp.sum(inv_cube * sep_z, axis=0),
            jnp.sum(inv_cube * (rel_x - radial * sep_x), axis=0),
            jnp.sum(inv_cube * (rel_y - radial * sep_y), axis=0),
            jnp.sum(inv_cube * (rel_z - radial * sep_z), axis=0),
        ],
        axis=0,
    )


def star_terms(predicted):
    position = predicted[0:3]
    velocity = predicted[3:6]
    inv_r = lax.rsqrt(jnp.sum(position * position, axis=0))
    inv_cube = inv_r * inv_r * inv_r
    radial = 3.0 * jnp.sum(position * velocity, axis=0) * inv_r * inv_r
    accel = -inv_cube[None, :] * position
    jerk_star = -inv_cube[None, :] * (velocity - radial[None, :] * position)
    return jnp.concatenate([accel, jerk_star], axis=0)


def correct(phase_space, derivatives, fresh, elapsed):
    half_dt = 0.5 * elapsed
    twelfth = elapsed * elapsed / 12.0
    vel_new = (
        phase_space[3:6]
        + half_dt * (derivatives[0:3] + fresh[0:3])
        + twelfth * (derivatives[3:6] - fresh[3:6])
    )
    pos_new = (
        phase_space[0:3]
        + half_dt * (phase_space[3:6] + vel_new)
        + twelfth * (derivatives[0:3] - fresh[0:3])
    )
    return jnp.concatenate([pos_new, vel_new], axis=0)


def _force_kernel(ctl_ref, tgt_ref, src_ref, mass_ref, out_ref):
    targets = tgt_ref.shape[2]
    for part in range(2):
        lo = ctl_ref[2 * part]
        hi = ctl_ref[2 * part + 1]

        def per_target(t, carry, part=part, lo=lo, hi=hi):
            tx = tgt_ref[part, 0, t]
            ty = tgt_ref[part, 1, t]
            tz = tgt_ref[part, 2, t]
            tu = tgt_ref[part, 3, t]
            tv = tgt_ref[part, 4, t]
            tw = tgt_ref[part, 5, t]

            def per_tile(s, acc):
                rows = pl.ds(pl.multiple_of(s * 8, 8), 8)
                sep_x = src_ref[0, rows, :] - tx
                sep_y = src_ref[1, rows, :] - ty
                sep_z = src_ref[2, rows, :] - tz
                rel_x = src_ref[3, rows, :] - tu
                rel_y = src_ref[4, rows, :] - tv
                rel_z = src_ref[5, rows, :] - tw
                dist_sq = sep_x * sep_x + sep_y * sep_y + sep_z * sep_z + soften_sq
                inv_r = lax.rsqrt(dist_sq)
                inv_sq = inv_r * inv_r
                inv_cube = mass_ref[rows, :] * inv_sq * inv_r
                radial = (sep_x * rel_x + sep_y * rel_y + sep_z * rel_z) * inv_sq
                pull_x = inv_cube * sep_x
                pull_y = inv_cube * sep_y
                pull_z = inv_cube * sep_z
                return (
                    acc[0] + pull_x,
                    acc[1] + pull_y,
                    acc[2] + pull_z,
                    acc[3] + inv_cube * rel_x,
                    acc[4] + inv_cube * rel_y,
                    acc[5] + inv_cube * rel_z,
                    acc[6] + radial * pull_x,
                    acc[7] + radial * pull_y,
                    acc[8] + radial * pull_z,
                )

            def per_group(g, acc):
                for k in range(GROUP):
                    acc = per_tile(g * GROUP + k, acc)
                return acc

            zero = jnp.zeros((8, 128), jnp.float32)
            acc = lax.fori_loop(lo, hi, per_group, (zero,) * 9)
            for k in range(9):
                out_ref[part, k, pl.ds(t, 1), :] = jnp.sum(acc[k], axis=0, keepdims=True)
            return carry

        lax.fori_loop(0, targets, per_target, 0)


def kernel_forces(ranges, targets, field, masses):
    out = pl.pallas_call(
        _force_kernel,
        out_shape=jax.ShapeDtypeStruct((2, 9, targets.shape[2], 128), jnp.float32),
        in_specs=[
            pl.BlockSpec(memory_space=pltpu.MemorySpace.SMEM),
            pl.BlockSpec(memory_space=pltpu.MemorySpace.SMEM),
            pl.BlockSpec(memory_space=pltpu.MemorySpace.VMEM),
            pl.BlockSpec(memory_space=pltpu.MemorySpace.VMEM),
        ],
        out_specs=pl.BlockSpec(memory_space=pltpu.MemorySpace.VMEM),
    )(ranges, targets, field, masses)
    sums = jnp.sum(out, axis=3)
    return jnp.concatenate([sums[:, 0:3], sums[:, 3:6] - 3.0 * sums[:, 6:9]], axis=1)


def shards(phase_space, derivatives, body_mass, active_lists):
    every = ("ia", "ja", "ha")
    plane = ("ja", "ha")
    local = jnp.concatenate([phase_space, derivatives, body_mass[None, :]], axis=0)
    local = local.reshape(13, local.shape[1] // BLK, BLK)
    full = lax.all_gather(local, plane, axis=1, tiled=True)
    block_total = full.shape[1]
    tiles = block_total // (8 * GROUP)
    slots = active_lists.shape[1] * active_lists.shape[2]
    devices = lax.axis_size("ia") * lax.axis_size("ja") * lax.axis_size("ha")
    my_unit = (
        lax.axis_index("ia") * lax.axis_size("ja") + lax.axis_index("ja")
    ) * lax.axis_size("ha") + lax.axis_index("ha")
    all_blocks = jnp.arange(block_total, dtype=jnp.int32)
    units = jnp.arange(devices, dtype=jnp.int32)
    last_blk = jnp.zeros((block_total,), jnp.float32)
    flat = active_lists.reshape(active_lists.shape[0], -1)
    live = flat >= 0
    live_count = jnp.sum(live.astype(jnp.int32), axis=1, keepdims=True)
    rank = jnp.cumsum(live.astype(jnp.int32), axis=1) - 1
    picks = (rank[:, :, None] == units[None, None, :slots]) & live[:, :, None]
    compact = jnp.sum(jnp.where(picks, flat[:, :, None], 0), axis=1)
    work = live_count * tiles
    share = (work + devices - 1) // devices
    begin = jnp.minimum(units[None, :] * share, work)
    finish = jnp.minimum(begin + share, work)
    job_a = jnp.minimum(begin // tiles, slots - 1)
    lo_a = begin - job_a * tiles
    hi_a = jnp.maximum(jnp.minimum(finish - job_a * tiles, tiles), lo_a)
    job_b = jnp.minimum(job_a + 1, slots - 1)
    hi_b = jnp.clip(finish - (job_a + 1) * tiles, 0, tiles)
    owner_a = jnp.where(hi_a > lo_a, jnp.take_along_axis(compact, job_a, axis=1), -1)
    owner_b = jnp.where(hi_b > 0, jnp.take_along_axis(compact, job_b, axis=1), -1)
    owner_all = jnp.stack([owner_a, owner_b], axis=2).reshape(flat.shape[0], -1)
    onehots = (all_blocks[None, :, None] == owner_all[:, None, :]).astype(jnp.float32)
    active_all = jnp.any(flat[:, :, None] == all_blocks[None, None, :], axis=1)
    mine = lambda x: lax.dynamic_index_in_dim(x, my_unit, 1, keepdims=False)
    ranges_all = jnp.stack(
        [mine(lo_a), mine(hi_a), jnp.zeros_like(mine(hi_b)), mine(hi_b)], axis=1
    ).astype(jnp.int32)
    ids_all = jnp.clip(
        jnp.stack(
            [
                jnp.take_along_axis(compact, mine(job_a)[:, None], axis=1)[:, 0],
                jnp.take_along_axis(compact, mine(job_b)[:, None], axis=1)[:, 0],
            ],
            axis=1,
        ),
        0,
        block_total - 1,
    )
    plans = (ranges_all, ids_all, onehots, active_all)
    plans, full = lax.optimization_barrier((plans, full))
    ranges_all, ids_all, onehots, active_all = plans
    mass = full[12]
    phase = full[0:6]
    deriv = full[6:12]
    for step_index in range(STEPS):
        now_time = (step_index + 1) * time_step
        ranges = ranges_all[step_index]
        id_a = ids_all[step_index, 0]
        id_b = ids_all[step_index, 1]
        onehot = onehots[step_index]
        active_flags = active_all[step_index]
        elapsed_blk = now_time - last_blk
        elapsed = elapsed_blk[None, :, None]
        predicted = predict(phase, deriv, elapsed)
        targets = jnp.stack(
            [
                lax.dynamic_index_in_dim(predicted, id_a, 1, keepdims=False),
                lax.dynamic_index_in_dim(predicted, id_b, 1, keepdims=False),
            ]
        )
        partial = kernel_forces(ranges, targets, predicted, mass)
        sent = jnp.broadcast_to(partial[None], (devices,) + partial.shape)
        got = lax.all_to_all(sent, every, 0, 0, tiled=True)
        later, _ = lax.optimization_barrier((predicted, partial))
        if step_index == STEPS - 1:
            break
        mutual = jnp.einsum(
            "bup,upcl->cbl", onehot.reshape(block_total, devices, 2), got,
            precision=lax.Precision.HIGHEST, preferred_element_type=jnp.float32,
        )
        fresh = mutual + star_terms(later)
        corrected = correct(phase, deriv, fresh, elapsed)
        active = active_flags[None, :, None]
        phase = jnp.where(active, corrected, phase)
        deriv = jnp.where(active, fresh, deriv)
        last_blk = jnp.where(active_flags, jnp.float32(now_time), last_blk)
    local_count = phase_space.shape[1]
    local_blocks = local_count // BLK
    offset = (lax.axis_index("ja") * lax.axis_size("ha") + lax.axis_index("ha")) * local_blocks
    own = lambda x: lax.dynamic_slice_in_dim(x, offset, local_blocks, axis=1)
    mutual = jnp.einsum(
        "bup,upcl->cbl",
        lax.dynamic_slice_in_dim(onehot, offset, local_blocks, axis=0).reshape(local_blocks, devices, 2),
        got,
        precision=lax.Precision.HIGHEST, preferred_element_type=jnp.float32,
    )
    own_phase = own(phase)
    own_deriv = own(deriv)
    own_elapsed = own(elapsed)
    fresh = mutual + star_terms(own(later))
    corrected = correct(own_phase, own_deriv, fresh, own_elapsed)
    active = lax.dynamic_slice_in_dim(active_flags, offset, local_blocks)[None, :, None]
    phase_out = jnp.where(active, corrected, own_phase)
    deriv_out = jnp.where(active, fresh, own_deriv)
    return (phase_out.reshape(6, local_count), deriv_out.reshape(6, local_count))


def solution(mesh):
    return jax.shard_map(
        shards,
        mesh=mesh,
        in_specs=(P(None, ("ja", "ha")), P(None, ("ja", "ha")), P(("ja", "ha")), P()),
        out_specs=(P(None, ("ja", "ha")), P(None, ("ja", "ha"))),
        check_vma=False,
    )
```

```python
import math

import jax
import jax.numpy as jnp
from jax import lax
from jax.sharding import PartitionSpec as P
from jax.experimental import pallas as pl
from jax.experimental.pallas import tpu as pltpu
from jax.experimental import pallas as pl
from jax.experimental.pallas import tpu as pltpu

BLK = 128
GROUP = 8
STEPS = 4


time_step = 0.02
soften_sq = 0.0025


def predict(phase_space, derivatives, elapsed):
    position = phase_space[0:3]
    velocity = phase_space[3:6]
    acceleration = derivatives[0:3]
    jerk_old = derivatives[3:6]
    pos_next = position + elapsed * (
        velocity + elapsed * (acceleration * 0.5 + elapsed * jerk_old / 6.0)
    )
    vel_next = velocity + elapsed * (acceleration + elapsed * jerk_old * 0.5)
    return jnp.concatenate([pos_next, vel_next], axis=0)


def pair_terms(targets, field_rows, body_mass):
    sep_x = field_rows[0][:, None] - targets[0][None, :]
    sep_y = field_rows[1][:, None] - targets[1][None, :]
    sep_z = field_rows[2][:, None] - targets[2][None, :]
    rel_x = field_rows[3][:, None] - targets[3][None, :]
    rel_y = field_rows[4][:, None] - targets[4][None, :]
    rel_z = field_rows[5][:, None] - targets[5][None, :]
    dist_sq = sep_x * sep_x + sep_y * sep_y + sep_z * sep_z + soften_sq
    inv_r = lax.rsqrt(dist_sq)
    inv_cube = body_mass[:, None] * inv_r * inv_r * inv_r
    radial = 3.0 * (sep_x * rel_x + sep_y * rel_y + sep_z * rel_z) * inv_r * inv_r
    return jnp.stack(
        [
            jnp.sum(inv_cube * sep_x, axis=0),
            jnp.sum(inv_cube * sep_y, axis=0),
            jnp.sum(inv_cube * sep_z, axis=0),
            jnp.sum(inv_cube * (rel_x - radial * sep_x), axis=0),
            jnp.sum(inv_cube * (rel_y - radial * sep_y), axis=0),
            jnp.sum(inv_cube * (rel_z - radial * sep_z), axis=0),
        ],
        axis=0,
    )


def star_terms(predicted):
    position = predicted[0:3]
    velocity = predicted[3:6]
    inv_r = lax.rsqrt(jnp.sum(position * position, axis=0))
    inv_cube = inv_r * inv_r * inv_r
    radial = 3.0 * jnp.sum(position * velocity, axis=0) * inv_r * inv_r
    accel = -inv_cube[None, :] * position
    jerk_star = -inv_cube[None, :] * (velocity - radial[None, :] * position)
    return jnp.concatenate([accel, jerk_star], axis=0)


def correct(phase_space, derivatives, fresh, elapsed):
    half_dt = 0.5 * elapsed
    twelfth = elapsed * elapsed / 12.0
    vel_new = (
        phase_space[3:6]
        + half_dt * (derivatives[0:3] + fresh[0:3])
        + twelfth * (derivatives[3:6] - fresh[3:6])
    )
    pos_new = (
        phase_space[0:3]
        + half_dt * (phase_space[3:6] + vel_new)
        + twelfth * (derivatives[0:3] - fresh[0:3])
    )
    return jnp.concatenate([pos_new, vel_new], axis=0)


def _force_kernel(ctl_ref, tgt_ref, src_ref, mass_ref, out_ref):
    targets = tgt_ref.shape[2]
    for part in range(2):
        lo = ctl_ref[2 * part]
        hi = ctl_ref[2 * part + 1]

        def per_target(t, carry, part=part, lo=lo, hi=hi):
            tx = tgt_ref[part, 0, t]
            ty = tgt_ref[part, 1, t]
            tz = tgt_ref[part, 2, t]
            tu = tgt_ref[part, 3, t]
            tv = tgt_ref[part, 4, t]
            tw = tgt_ref[part, 5, t]

            def per_tile(s, acc):
                rows = pl.ds(pl.multiple_of(s * 8, 8), 8)
                sep_x = src_ref[0, rows, :] - tx
                sep_y = src_ref[1, rows, :] - ty
                sep_z = src_ref[2, rows, :] - tz
                rel_x = src_ref[3, rows, :] - tu
                rel_y = src_ref[4, rows, :] - tv
                rel_z = src_ref[5, rows, :] - tw
                dist_sq = sep_x * sep_x + sep_y * sep_y + sep_z * sep_z + soften_sq
                inv_r = lax.rsqrt(dist_sq)
                inv_sq = inv_r * inv_r
                inv_cube = mass_ref[rows, :] * inv_sq * inv_r
                radial = (sep_x * rel_x + sep_y * rel_y + sep_z * rel_z) * inv_sq
                pull_x = inv_cube * sep_x
                pull_y = inv_cube * sep_y
                pull_z = inv_cube * sep_z
                return (
                    acc[0] + pull_x,
                    acc[1] + pull_y,
                    acc[2] + pull_z,
                    acc[3] + inv_cube * rel_x,
                    acc[4] + inv_cube * rel_y,
                    acc[5] + inv_cube * rel_z,
                    acc[6] + radial * pull_x,
                    acc[7] + radial * pull_y,
                    acc[8] + radial * pull_z,
                )

            def per_group(g, acc):
                for k in range(GROUP):
                    acc = per_tile(g * GROUP + k, acc)
                return acc

            zero = jnp.zeros((8, 128), jnp.float32)
            acc = lax.fori_loop(lo, hi, per_group, (zero,) * 9)
            for k in range(9):
                out_ref[part, k, pl.ds(t, 1), :] = jnp.sum(acc[k], axis=0, keepdims=True)
            return carry

        @pl.when(hi > lo)
        def _(per_target=per_target):
            lax.fori_loop(0, targets, per_target, 0)

        @pl.when(hi <= lo)
        def _(part=part):
            out_ref[part] = jnp.zeros(out_ref.shape[1:], out_ref.dtype)


def kernel_forces(ranges, targets, field, masses):
    out = pl.pallas_call(
        _force_kernel,
        out_shape=jax.ShapeDtypeStruct((2, 9, targets.shape[2], 128), jnp.float32),
        in_specs=[
            pl.BlockSpec(memory_space=pltpu.MemorySpace.SMEM),
            pl.BlockSpec(memory_space=pltpu.MemorySpace.SMEM),
            pl.BlockSpec(memory_space=pltpu.MemorySpace.VMEM),
            pl.BlockSpec(memory_space=pltpu.MemorySpace.VMEM),
        ],
        out_specs=pl.BlockSpec(memory_space=pltpu.MemorySpace.VMEM),
    )(ranges, targets, field, masses)
    sums = jnp.sum(out, axis=3)
    return jnp.concatenate([sums[:, 0:3], sums[:, 3:6] - 3.0 * sums[:, 6:9]], axis=1)


def shards(phase_space, derivatives, body_mass, active_lists):
    every = ("ia", "ja", "ha")
    plane = ("ja", "ha")
    local = jnp.concatenate([phase_space, derivatives, body_mass[None, :]], axis=0)
    local = local.reshape(13, local.shape[1] // BLK, BLK)
    full = lax.all_gather(local, plane, axis=1, tiled=True)
    block_total = full.shape[1]
    tiles = block_total // (8 * GROUP)
    slots = active_lists.shape[1] * active_lists.shape[2]
    devices = lax.axis_size("ia") * lax.axis_size("ja") * lax.axis_size("ha")
    my_unit = (
        lax.axis_index("ia") * lax.axis_size("ja") + lax.axis_index("ja")
    ) * lax.axis_size("ha") + lax.axis_index("ha")
    all_blocks = jnp.arange(block_total, dtype=jnp.int32)
    units = jnp.arange(devices, dtype=jnp.int32)
    last_blk = jnp.zeros((block_total,), jnp.float32)
    flat = active_lists.reshape(active_lists.shape[0], -1)
    live = flat >= 0
    live_count = jnp.sum(live.astype(jnp.int32), axis=1, keepdims=True)
    rank = jnp.cumsum(live.astype(jnp.int32), axis=1) - 1
    picks = (rank[:, :, None] == units[None, None, :slots]) & live[:, :, None]
    compact = jnp.sum(jnp.where(picks, flat[:, :, None], 0), axis=1)
    work = live_count * tiles
    share = (work + devices - 1) // devices
    begin = jnp.minimum(units[None, :] * share, work)
    finish = jnp.minimum(begin + share, work)
    job_a = jnp.minimum(begin // tiles, slots - 1)
    lo_a = begin - job_a * tiles
    hi_a = jnp.maximum(jnp.minimum(finish - job_a * tiles, tiles), lo_a)
    job_b = jnp.minimum(job_a + 1, slots - 1)
    hi_b = jnp.clip(finish - (job_a + 1) * tiles, 0, tiles)
    owner_a = jnp.where(hi_a > lo_a, jnp.take_along_axis(compact, job_a, axis=1), -1)
    owner_b = jnp.where(hi_b > 0, jnp.take_along_axis(compact, job_b, axis=1), -1)
    owner_all = jnp.stack([owner_a, owner_b], axis=2).reshape(flat.shape[0], -1)
    onehots = (all_blocks[None, :, None] == owner_all[:, None, :]).astype(jnp.float32)
    active_all = jnp.any(flat[:, :, None] == all_blocks[None, None, :], axis=1)
    mine = lambda x: lax.dynamic_index_in_dim(x, my_unit, 1, keepdims=False)
    ranges_all = jnp.stack(
        [mine(lo_a), mine(hi_a), jnp.zeros_like(mine(hi_b)), mine(hi_b)], axis=1
    ).astype(jnp.int32)
    ids_all = jnp.clip(
        jnp.stack(
            [
                jnp.take_along_axis(compact, mine(job_a)[:, None], axis=1)[:, 0],
                jnp.take_along_axis(compact, mine(job_b)[:, None], axis=1)[:, 0],
            ],
            axis=1,
        ),
        0,
        block_total - 1,
    )
    plans = (ranges_all, ids_all, onehots, active_all)
    plans, full = lax.optimization_barrier((plans, full))
    ranges_all, ids_all, onehots, active_all = plans
    mass = full[12]
    phase = full[0:6]
    deriv = full[6:12]
    for step_index in range(STEPS):
        now_time = (step_index + 1) * time_step
        ranges = ranges_all[step_index]
        id_a = ids_all[step_index, 0]
        id_b = ids_all[step_index, 1]
        onehot = onehots[step_index]
        active_flags = active_all[step_index]
        elapsed_blk = now_time - last_blk
        elapsed = elapsed_blk[None, :, None]
        predicted = predict(phase, deriv, elapsed)
        targets = jnp.stack(
            [
                lax.dynamic_index_in_dim(predicted, id_a, 1, keepdims=False),
                lax.dynamic_index_in_dim(predicted, id_b, 1, keepdims=False),
            ]
        )
        partial = kernel_forces(ranges, targets, predicted, mass)
        sent = jnp.broadcast_to(partial[None], (devices,) + partial.shape)
        got = lax.all_to_all(sent, every, 0, 0, tiled=True)
        later, _ = lax.optimization_barrier((predicted, partial))
        if step_index == STEPS - 1:
            break
        mutual = jnp.einsum(
            "bup,upcl->cbl", onehot.reshape(block_total, devices, 2), got,
            precision=lax.Precision.HIGHEST, preferred_element_type=jnp.float32,
        )
        fresh = mutual + star_terms(later)
        corrected = correct(phase, deriv, fresh, elapsed)
        active = active_flags[None, :, None]
        phase = jnp.where(active, corrected, phase)
        deriv = jnp.where(active, fresh, deriv)
        last_blk = jnp.where(active_flags, jnp.float32(now_time), last_blk)
    local_count = phase_space.shape[1]
    local_blocks = local_count // BLK
    offset = (lax.axis_index("ja") * lax.axis_size("ha") + lax.axis_index("ha")) * local_blocks
    own = lambda x: lax.dynamic_slice_in_dim(x, offset, local_blocks, axis=1)
    mutual = jnp.einsum(
        "bup,upcl->cbl",
        lax.dynamic_slice_in_dim(onehot, offset, local_blocks, axis=0).reshape(local_blocks, devices, 2),
        got,
        precision=lax.Precision.HIGHEST, preferred_element_type=jnp.float32,
    )
    own_phase = own(phase)
    own_deriv = own(deriv)
    own_elapsed = own(elapsed)
    fresh = mutual + star_terms(own(later))
    corrected = correct(own_phase, own_deriv, fresh, own_elapsed)
    active = lax.dynamic_slice_in_dim(active_flags, offset, local_blocks)[None, :, None]
    phase_out = jnp.where(active, corrected, own_phase)
    deriv_out = jnp.where(active, fresh, own_deriv)
    return (phase_out.reshape(6, local_count), deriv_out.reshape(6, local_count))


def solution(mesh):
    return jax.shard_map(
        shards,
        mesh=mesh,
        in_specs=(P(None, ("ja", "ha")), P(None, ("ja", "ha")), P(("ja", "ha")), P()),
        out_specs=(P(None, ("ja", "ha")), P(None, ("ja", "ha"))),
        check_vma=False,
    )
```

```python
import math

import jax
import jax.numpy as jnp
from jax import lax
from jax.sharding import PartitionSpec as P
from jax.experimental import pallas as pl
from jax.experimental.pallas import tpu as pltpu
from jax.experimental import pallas as pl
from jax.experimental.pallas import tpu as pltpu

BLK = 128
GROUP = 8
STEPS = 4


time_step = 0.02
soften_sq = 0.0025


def predict(phase_space, derivatives, elapsed):
    position = phase_space[0:3]
    velocity = phase_space[3:6]
    acceleration = derivatives[0:3]
    jerk_old = derivatives[3:6]
    pos_next = position + elapsed * (
        velocity + elapsed * (acceleration * 0.5 + elapsed * jerk_old / 6.0)
    )
    vel_next = velocity + elapsed * (acceleration + elapsed * jerk_old * 0.5)
    return jnp.concatenate([pos_next, vel_next], axis=0)


def pair_terms(targets, field_rows, body_mass):
    sep_x = field_rows[0][:, None] - targets[0][None, :]
    sep_y = field_rows[1][:, None] - targets[1][None, :]
    sep_z = field_rows[2][:, None] - targets[2][None, :]
    rel_x = field_rows[3][:, None] - targets[3][None, :]
    rel_y = field_rows[4][:, None] - targets[4][None, :]
    rel_z = field_rows[5][:, None] - targets[5][None, :]
    dist_sq = sep_x * sep_x + sep_y * sep_y + sep_z * sep_z + soften_sq
    inv_r = lax.rsqrt(dist_sq)
    inv_cube = body_mass[:, None] * inv_r * inv_r * inv_r
    radial = 3.0 * (sep_x * rel_x + sep_y * rel_y + sep_z * rel_z) * inv_r * inv_r
    return jnp.stack(
        [
            jnp.sum(inv_cube * sep_x, axis=0),
            jnp.sum(inv_cube * sep_y, axis=0),
            jnp.sum(inv_cube * sep_z, axis=0),
            jnp.sum(inv_cube * (rel_x - radial * sep_x), axis=0),
            jnp.sum(inv_cube * (rel_y - radial * sep_y), axis=0),
            jnp.sum(inv_cube * (rel_z - radial * sep_z), axis=0),
        ],
        axis=0,
    )


def star_terms(predicted):
    position = predicted[0:3]
    velocity = predicted[3:6]
    inv_r = lax.rsqrt(jnp.sum(position * position, axis=0))
    inv_cube = inv_r * inv_r * inv_r
    radial = 3.0 * jnp.sum(position * velocity, axis=0) * inv_r * inv_r
    accel = -inv_cube[None, :] * position
    jerk_star = -inv_cube[None, :] * (velocity - radial[None, :] * position)
    return jnp.concatenate([accel, jerk_star], axis=0)


def correct(phase_space, derivatives, fresh, elapsed):
    half_dt = 0.5 * elapsed
    twelfth = elapsed * elapsed / 12.0
    vel_new = (
        phase_space[3:6]
        + half_dt * (derivatives[0:3] + fresh[0:3])
        + twelfth * (derivatives[3:6] - fresh[3:6])
    )
    pos_new = (
        phase_space[0:3]
        + half_dt * (phase_space[3:6] + vel_new)
        + twelfth * (derivatives[0:3] - fresh[0:3])
    )
    return jnp.concatenate([pos_new, vel_new], axis=0)


def _force_kernel(ctl_ref, tgt_ref, src_ref, mass_ref, out_ref):
    targets = tgt_ref.shape[2]
    for part in range(2):
        lo = ctl_ref[2 * part]
        hi = ctl_ref[2 * part + 1]

        def per_target(t, carry, part=part, lo=lo, hi=hi):
            tx = tgt_ref[part, 0, t]
            ty = tgt_ref[part, 1, t]
            tz = tgt_ref[part, 2, t]
            tu = tgt_ref[part, 3, t]
            tv = tgt_ref[part, 4, t]
            tw = tgt_ref[part, 5, t]

            def per_tile(s, acc):
                rows = pl.ds(pl.multiple_of(s * 8, 8), 8)
                sep_x = src_ref[0, rows, :] - tx
                sep_y = src_ref[1, rows, :] - ty
                sep_z = src_ref[2, rows, :] - tz
                rel_x = src_ref[3, rows, :] - tu
                rel_y = src_ref[4, rows, :] - tv
                rel_z = src_ref[5, rows, :] - tw
                dist_sq = sep_x * sep_x + sep_y * sep_y + sep_z * sep_z + soften_sq
                inv_r = lax.rsqrt(dist_sq)
                inv_sq = inv_r * inv_r
                inv_cube = mass_ref[rows, :] * inv_sq * inv_r
                radial = (sep_x * rel_x + sep_y * rel_y + sep_z * rel_z) * inv_sq
                pull_x = inv_cube * sep_x
                pull_y = inv_cube * sep_y
                pull_z = inv_cube * sep_z
                return (
                    acc[0] + pull_x,
                    acc[1] + pull_y,
                    acc[2] + pull_z,
                    acc[3] + inv_cube * rel_x,
                    acc[4] + inv_cube * rel_y,
                    acc[5] + inv_cube * rel_z,
                    acc[6] + radial * pull_x,
                    acc[7] + radial * pull_y,
                    acc[8] + radial * pull_z,
                )

            def per_group(g, acc):
                for k in range(GROUP):
                    acc = per_tile(g * GROUP + k, acc)
                return acc

            zero = jnp.zeros((8, 128), jnp.float32)
            acc = lax.fori_loop(lo, hi, per_group, (zero,) * 9)
            for k in range(9):
                out_ref[part, k, pl.ds(t, 1), :] = jnp.sum(acc[k], axis=0, keepdims=True)
            return carry

        lax.fori_loop(0, targets, per_target, 0)


def kernel_forces(ranges, targets, field, masses):
    out = pl.pallas_call(
        _force_kernel,
        out_shape=jax.ShapeDtypeStruct((2, 9, targets.shape[2], 128), jnp.float32),
        in_specs=[
            pl.BlockSpec(memory_space=pltpu.MemorySpace.SMEM),
            pl.BlockSpec(memory_space=pltpu.MemorySpace.SMEM),
            pl.BlockSpec(memory_space=pltpu.MemorySpace.VMEM),
            pl.BlockSpec(memory_space=pltpu.MemorySpace.VMEM),
        ],
        out_specs=pl.BlockSpec(memory_space=pltpu.MemorySpace.VMEM),
    )(ranges, targets, field, masses)
    sums = jnp.sum(out, axis=3)
    return jnp.concatenate([sums[:, 0:3], sums[:, 3:6] - 3.0 * sums[:, 6:9]], axis=1)


def shards(phase_space, derivatives, body_mass, active_lists):
    every = ("ia", "ja", "ha")
    plane = ("ja", "ha")
    local = jnp.concatenate([phase_space, derivatives, body_mass[None, :]], axis=0)
    local = local.reshape(13, local.shape[1] // BLK, BLK)
    full = lax.all_gather(local, plane, axis=1, tiled=True)
    block_total = full.shape[1]
    tiles = block_total // (8 * GROUP)
    slots = active_lists.shape[1] * active_lists.shape[2]
    devices = lax.axis_size("ia") * lax.axis_size("ja") * lax.axis_size("ha")
    my_unit = (
        lax.axis_index("ia") * lax.axis_size("ja") + lax.axis_index("ja")
    ) * lax.axis_size("ha") + lax.axis_index("ha")
    all_blocks = jnp.arange(block_total, dtype=jnp.int32)
    units = jnp.arange(devices, dtype=jnp.int32)
    last_blk = jnp.zeros((block_total,), jnp.float32)
    flat = active_lists.reshape(active_lists.shape[0], -1)
    live = flat >= 0
    live_count = jnp.sum(live.astype(jnp.int32), axis=1, keepdims=True)
    rank = jnp.cumsum(live.astype(jnp.int32), axis=1) - 1
    picks = (rank[:, :, None] == units[None, None, :slots]) & live[:, :, None]
    compact = jnp.sum(jnp.where(picks, flat[:, :, None], 0), axis=1)
    work = live_count * tiles
    share = (work + devices - 1) // devices
    begin = jnp.minimum(units[None, :] * share, work)
    finish = jnp.minimum(begin + share, work)
    job_a = jnp.minimum(begin // tiles, slots - 1)
    lo_a = begin - job_a * tiles
    hi_a = jnp.maximum(jnp.minimum(finish - job_a * tiles, tiles), lo_a)
    job_b = jnp.minimum(job_a + 1, slots - 1)
    hi_b = jnp.clip(finish - (job_a + 1) * tiles, 0, tiles)
    owner_a = jnp.where(hi_a > lo_a, jnp.take_along_axis(compact, job_a, axis=1), -1)
    owner_b = jnp.where(hi_b > 0, jnp.take_along_axis(compact, job_b, axis=1), -1)
    owner_all = jnp.stack([owner_a, owner_b], axis=2).reshape(flat.shape[0], -1)
    onehots = (all_blocks[None, :, None] == owner_all[:, None, :]).astype(jnp.float32)
    active_all = jnp.any(flat[:, :, None] == all_blocks[None, None, :], axis=1)
    mine = lambda x: lax.dynamic_index_in_dim(x, my_unit, 1, keepdims=False)
    ranges_all = jnp.stack(
        [mine(lo_a), mine(hi_a), jnp.zeros_like(mine(hi_b)), mine(hi_b)], axis=1
    ).astype(jnp.int32)
    ids_all = jnp.clip(
        jnp.stack(
            [
                jnp.take_along_axis(compact, mine(job_a)[:, None], axis=1)[:, 0],
                jnp.take_along_axis(compact, mine(job_b)[:, None], axis=1)[:, 0],
            ],
            axis=1,
        ),
        0,
        block_total - 1,
    )
    plans = (ranges_all, ids_all, onehots, active_all)
    plans, full = lax.optimization_barrier((plans, full))
    ranges_all, ids_all, onehots, active_all = plans
    mass = full[12]
    phase = full[0:6]
    deriv = full[6:12]
    for step_index in range(STEPS):
        now_time = (step_index + 1) * time_step
        ranges = ranges_all[step_index]
        id_a = ids_all[step_index, 0]
        id_b = ids_all[step_index, 1]
        onehot = onehots[step_index]
        active_flags = active_all[step_index]
        elapsed_blk = now_time - last_blk
        elapsed = elapsed_blk[None, :, None]
        predicted = lax.optimization_barrier(predict(phase, deriv, elapsed))
        targets = jnp.stack(
            [
                lax.dynamic_index_in_dim(predicted, id_a, 1, keepdims=False),
                lax.dynamic_index_in_dim(predicted, id_b, 1, keepdims=False),
            ]
        )
        partial = kernel_forces(ranges, targets, predicted, mass)
        sent = jnp.broadcast_to(partial[None], (devices,) + partial.shape)
        got = lax.all_to_all(sent, every, 0, 0, tiled=True)
        later, _ = lax.optimization_barrier((predicted, partial))
        if step_index == STEPS - 1:
            break
        mutual = jnp.einsum(
            "bup,upcl->cbl", onehot.reshape(block_total, devices, 2), got,
            precision=lax.Precision.HIGHEST, preferred_element_type=jnp.float32,
        )
        fresh = mutual + star_terms(later)
        corrected = correct(phase, deriv, fresh, elapsed)
        active = active_flags[None, :, None]
        phase = jnp.where(active, corrected, phase)
        deriv = jnp.where(active, fresh, deriv)
        last_blk = jnp.where(active_flags, jnp.float32(now_time), last_blk)
    local_count = phase_space.shape[1]
    local_blocks = local_count // BLK
    offset = (lax.axis_index("ja") * lax.axis_size("ha") + lax.axis_index("ha")) * local_blocks
    own = lambda x: lax.dynamic_slice_in_dim(x, offset, local_blocks, axis=1)
    mutual = jnp.einsum(
        "bup,upcl->cbl",
        lax.dynamic_slice_in_dim(onehot, offset, local_blocks, axis=0).reshape(local_blocks, devices, 2),
        got,
        precision=lax.Precision.HIGHEST, preferred_element_type=jnp.float32,
    )
    own_phase = own(phase)
    own_deriv = own(deriv)
    own_elapsed = own(elapsed)
    fresh = mutual + star_terms(own(later))
    corrected = correct(own_phase, own_deriv, fresh, own_elapsed)
    active = lax.dynamic_slice_in_dim(active_flags, offset, local_blocks)[None, :, None]
    phase_out = jnp.where(active, corrected, own_phase)
    deriv_out = jnp.where(active, fresh, own_deriv)
    return (phase_out.reshape(6, local_count), deriv_out.reshape(6, local_count))


def solution(mesh):
    return jax.shard_map(
        shards,
        mesh=mesh,
        in_specs=(P(None, ("ja", "ha")), P(None, ("ja", "ha")), P(("ja", "ha")), P()),
        out_specs=(P(None, ("ja", "ha")), P(None, ("ja", "ha"))),
        check_vma=False,
    )
```
